32 devices in a mesh: pair: 4 (over x, core), blk: 8 (over z, y).
Axes of the slice: x: 2, y: 2, z: 4, core: 2. Of those that a mesh axis runs over, the one named last changes fastest.
Arguments:
- left_feats: bfloat16 [4, 64, 256, 256], P('pair', None, 'blk'), may hold values from -6 to 6
- right_feats: bfloat16 [4, 64, 256, 256], P('pair', None, 'blk'), may hold values from -6 to 6
- offsets: int32 [8], P('blk'), may hold values from 0 to 3, as said below
- hidden: bfloat16 [4, 64, 256, 128], P('pair', None, 'blk'), may hold values from -1 to 1
- context: bfloat16 [4, 3, 64, 256, 128], P('pair', None, None, 'blk'), may hold values from -6 to 6
- gru_weights: bfloat16 [2, 3, 5, 164, 128], replicated, may hold values from -0.21875 to 0.21875
- hidden_grad: float32 [4, 64, 256, 128], P('pair', None, 'blk'), may hold values from -0.06 to 0.06
Outputs:
- new_hidden: bfloat16 [4, 64, 256, 128], P('pair', None, 'blk')
- weight_grads: float32 [2, 3, 5, 164, 128], replicated
- hidden_in_grad: float32 [4, 64, 256, 128], P('pair', None, 'blk')
The draws below stay inside these ranges and needn't reach their ends.
Inputs may be any that keep to these rules, and one draw needn't show every extreme that they name: Stripe s reads the frame-2 blocks s - offsets[s] - 1 and s - offsets[s]; some stripe has offset 4 - 1.
All inputs are finite; a program needn't handle non-finite values.
Results may differ from the reference program's by a relative error of at most 0.0054.
Values may be sent and summed in bfloat16 or wider, within the bound.
A program may use at most 128 MiB of HBM per device.

```python
import functools
import math
import jax
import jax.numpy as jnp
import numpy as np
from jax import lax

C = 256
HD = 128
LEVELS = 4
RADIUS = 4
KS = 5
BAND = 4
ROWS = 64
COLS = 32
CORR = 36
STRIPES = 8
WIDTH = 256
PAIRS = 4


def draw_offsets(key, part):
    first_key, second_key = jax.random.split(jax.random.fold_in(key, 17))
    values = jax.random.randint(first_key, (STRIPES,), 0, BAND, dtype=jnp.int32)
    chosen = jax.random.randint(second_key, (), 0, STRIPES, dtype=jnp.int32)
    return jnp.where(jnp.arange(STRIPES, dtype=jnp.int32) == chosen, BAND - 1, values).astype(jnp.int32)


def level_of(stream_key, dims, pieces, low, high):
    loudness = 1.0
    for position, shards_of in pieces:
        heights = jax.random.uniform(jax.random.fold_in(jax.random.fold_in(stream_key, 6), position), (shards_of,), jnp.float32, low / len(pieces), high / len(pieces))
        loudness = loudness * jnp.repeat(jnp.exp(heights), dims[position] // shards_of).reshape((-1,) + (1,) * (len(dims) - 1 - position))
    return loudness


def normal_values(rng, shape, width, most, cuts=(), kind=jnp.bfloat16):
    factor_of = level_of(rng, shape, cuts, -0.22, 0.18) if cuts else 1.0
    entries = jax.random.normal(rng, shape, jnp.float32) * width * factor_of
    return jnp.minimum(jnp.maximum(entries, -most), most).astype(kind)


def setup_inputs(seed: int = 0) -> dict:
    splits = jax.random.split(jax.random.key(seed), 8)
    return {
        "left_feats": normal_values(splits[0], (PAIRS, ROWS, WIDTH, C), 1.0, 6.0, ((0, 4), (2, 8))),
        "right_feats": normal_values(splits[1], (PAIRS, ROWS, WIDTH, C), 1.0, 6.0, ((0, 4), (2, 8))),
        "offsets": draw_offsets(jax.random.fold_in(splits[7], 71), 0),
        "hidden": jnp.clip(jax.random.uniform(splits[3], (PAIRS, ROWS, WIDTH, HD), jnp.float32, -1.0, 1.0) * level_of(splits[3], (PAIRS, ROWS, WIDTH, HD), ((0, 4), (2, 8)), -0.4, 0.0), -1.0, 1.0).astype(jnp.bfloat16),
        "context": normal_values(splits[4], (PAIRS, 3, ROWS, WIDTH, HD), 1.0, 6.0, ((0, 4), (3, 8))),
        "gru_weights": normal_values(splits[5], (2, 3, KS, HD + CORR, HD), (KS * (HD + CORR)) ** -0.5, 0.21875),
        "hidden_grad": normal_values(splits[6], (PAIRS, ROWS, WIDTH, HD), 0.01, 0.06, ((0, 4), (2, 8)), jnp.float32),
    }


def lookup_table(column_count, level_count, radius_len):
    tap_count = 2 * radius_len + 1
    lookup = np.zeros((column_count, 2 * column_count, level_count * tap_count), np.float32)
    positions = np.arange(column_count)
    for level_id in range(level_count):
        pool_span = 2 ** level_id
        pooled_cols = 2 * column_count // pool_span
        for tap_id in range(tap_count):
            centre = (positions + column_count // 2) // pool_span + tap_id - radius_len
            inside = (centre >= 0) & (centre < pooled_cols)
            for inner_id in range(pool_span):
                lookup[positions[inside], centre[inside] * pool_span + inner_id, level_id * tap_count + tap_id] = 1.0 / pool_span
    return lookup

def tap_stack(padded, extent, axis_dim, kernel_len):
    return jnp.concatenate([lax.slice_in_dim(padded, tap_id, tap_id + extent, axis=axis_dim) for tap_id in range(kernel_len)], axis=-1)

def conv_apply(padded, weight_taps, extent, axis_dim):
    kernel_len, in_chan, out_chan = weight_taps.shape
    stacked = tap_stack(padded, extent, axis_dim, kernel_len)
    flat_taps = stacked.reshape(-1, kernel_len * in_chan)
    result = jnp.dot(flat_taps, weight_taps.reshape(kernel_len * in_chan, out_chan), preferred_element_type=jnp.float32)
    return result.reshape(stacked.shape[:-1] + (out_chan,))

def conv_weight_grad(padded, deltas, axis_dim):
    extent = deltas.shape[axis_dim]
    kernel_len = padded.shape[axis_dim] - extent + 1
    stacked = tap_stack(padded, extent, axis_dim, kernel_len)
    flat_taps = stacked.reshape(-1, stacked.shape[-1])
    flat_deltas = deltas.reshape(-1, deltas.shape[-1])
    result = lax.dot_general(flat_taps, flat_deltas, (((0,), (0,)), ((), ())), preferred_element_type=jnp.float32)
    return result.reshape(kernel_len, padded.shape[-1], deltas.shape[-1])

def conv_input_grad(deltas, weight_taps, axis_dim):
    kernel_len, in_chan, out_chan = weight_taps.shape
    backward_taps = lax.dot_general(deltas.reshape(-1, out_chan), weight_taps.reshape(kernel_len * in_chan, out_chan), (((1,), (1,)), ((), ())), preferred_element_type=jnp.float32)
    backward_taps = backward_taps.reshape(deltas.shape[:-1] + (kernel_len * in_chan,))
    summed = None
    for tap_id in range(kernel_len):
        tap_part = backward_taps[..., tap_id * in_chan:(tap_id + 1) * in_chan]
        widths = [(0, 0)] * deltas.ndim
        widths[axis_dim] = (tap_id, kernel_len - 1 - tap_id)
        shifted = jnp.pad(tap_part, widths)
        summed = shifted if summed is None else summed + shifted
    return summed

def pad_along(values, axis_dim):
    widths = [(0, 0)] * values.ndim
    widths[axis_dim] = (2, 2)
    return jnp.pad(values, widths)

def crop_along(values, axis_dim):
    extent = values.shape[axis_dim] - 4
    return lax.slice_in_dim(values, 2, extent + 2, axis=axis_dim)

def section_forward(padded, context_parts, weights, axis_dim, extend):
    extent = padded.shape[axis_dim] - 4
    hidden_width = weights.shape[-1]
    own_inputs = lax.slice_in_dim(padded, 2, extent + 2, axis=axis_dim)
    hidden_own = own_inputs[..., :hidden_width].astype(jnp.float32)
    feat_padded = padded[..., hidden_width:]
    update_gate = jax.nn.sigmoid(conv_apply(padded, weights[0], extent, axis_dim) + context_parts[0].astype(jnp.float32))
    reset_gate = jax.nn.sigmoid(conv_apply(padded, weights[1], extent, axis_dim) + context_parts[1].astype(jnp.float32))
    reset_hidden = (reset_gate * hidden_own).astype(jnp.bfloat16)
    gated_padded = jnp.concatenate([extend(reset_hidden), feat_padded], axis=-1)
    candidate = jnp.tanh(conv_apply(gated_padded, weights[2], extent, axis_dim) + context_parts[2].astype(jnp.float32))
    blended = (1.0 - update_gate) * hidden_own + update_gate * candidate
    return (blended, (update_gate, reset_gate, candidate, hidden_own, padded, gated_padded))

def section_backward(cotangent, stored, weights, axis_dim, fold_rims, want_hidden):
    update_gate, reset_gate, candidate, hidden_own, padded, gated_padded = stored
    hidden_width = weights.shape[-1]
    delta_cand = (cotangent * update_gate * (1.0 - candidate * candidate)).astype(jnp.bfloat16)
    grad_cand = conv_weight_grad(gated_padded, delta_cand, axis_dim)
    back_gated = fold_rims(conv_input_grad(delta_cand, weights[2][:, :hidden_width], axis_dim))
    delta_update = (cotangent * (candidate - hidden_own) * update_gate * (1.0 - update_gate)).astype(jnp.bfloat16)
    delta_reset = (back_gated * hidden_own * reset_gate * (1.0 - reset_gate)).astype(jnp.bfloat16)
    grad_update = conv_weight_grad(padded, delta_update, axis_dim)
    grad_reset = conv_weight_grad(padded, delta_reset, axis_dim)
    grad_stack = jnp.stack([grad_update, grad_reset, grad_cand])
    if want_hidden:
        back_inputs = conv_input_grad(delta_update, weights[0][:, :hidden_width], axis_dim) + conv_input_grad(delta_reset, weights[1][:, :hidden_width], axis_dim)
        hidden_back = cotangent * (1.0 - update_gate) + back_gated * reset_gate + fold_rims(back_inputs)
        return (grad_stack, hidden_back)
    return (grad_stack, None)

def reference(left_feats, right_feats, offsets, hidden, context, gru_weights, hidden_grad):
    lookup = jnp.asarray(lookup_table(COLS, LEVELS, RADIUS))
    inv_scale = 1.0 / math.sqrt(C)
    block_index = jnp.arange(STRIPES, dtype=jnp.int32) - offsets.astype(jnp.int32) + BAND
    outputs = []
    input_grads = []
    summed = jnp.zeros(gru_weights.shape, jnp.float32)
    for pair_index in range(PAIRS):
        left_rows = left_feats[pair_index].reshape(ROWS, STRIPES, COLS, C)
        blocks = right_feats[pair_index].reshape(ROWS, STRIPES, COLS, C)
        padded_blocks = jnp.concatenate([jnp.zeros((ROWS, BAND, COLS, C), jnp.bfloat16), blocks], axis=1)
        window = jnp.concatenate([jnp.take(padded_blocks, block_index - 1, axis=1), jnp.take(padded_blocks, block_index, axis=1)], axis=2)
        scores = jnp.einsum('hnxc,hnjc->hnxj', left_rows.astype(jnp.float32), window.astype(jnp.float32)) * inv_scale
        features = jnp.einsum('hnxj,xjf->hnxf', scores, lookup, precision=lax.Precision.HIGHEST)
        features = features.reshape(ROWS, WIDTH, CORR).astype(jnp.bfloat16)
        context_parts = context[pair_index]
        first_inputs = jnp.concatenate([hidden[pair_index], features], axis=-1)
        first_new, first_stored = section_forward(pad_along(first_inputs, 1), context_parts, gru_weights[0], 1, functools.partial(pad_along, axis_dim=1))
        first_hidden = first_new.astype(jnp.bfloat16)
        second_inputs = jnp.concatenate([first_hidden, features], axis=-1)
        second_new, second_stored = section_forward(pad_along(second_inputs, 0), context_parts, gru_weights[1], 0, functools.partial(pad_along, axis_dim=0))
        outputs.append(second_new.astype(jnp.bfloat16))
        second_grads, first_back = section_backward(hidden_grad[pair_index], second_stored, gru_weights[1], 0, functools.partial(crop_along, axis_dim=0), True)
        first_grads, hidden_back = section_backward(first_back, first_stored, gru_weights[0], 1, functools.partial(crop_along, axis_dim=1), True)
        input_grads.append(hidden_back)
        summed = summed + jnp.stack([first_grads, second_grads])
    return (jnp.stack(outputs), summed, jnp.stack(input_grads))
```

```python
import functools
import math

import jax
import jax.numpy as jnp
import numpy as np
from jax import lax
from jax.experimental import pallas as pl
from jax.experimental.pallas import tpu as pltpu
from jax.sharding import PartitionSpec as P

LEVELS = 4
RADIUS = 4


def with_halo(block, sides, width):
    for axis, dim in sides:
        count = lax.axis_size(axis)
        forward = [(i, i + 1) for i in range(count - 1)]
        backward = [(target, source) for source, target in forward]
        low = lax.ppermute(
            lax.slice_in_dim(block, block.shape[dim] - width, None, axis=dim), axis, forward
        )
        high = lax.ppermute(lax.slice_in_dim(block, 0, width, axis=dim), axis, backward)
        block = jnp.concatenate([low, block, high], axis=dim)
    return block


def lookup_table(column_count, level_count, radius_len):
    tap_count = 2 * radius_len + 1
    lookup = np.zeros((column_count, 2 * column_count, level_count * tap_count), np.float32)
    positions = np.arange(column_count)
    for level_id in range(level_count):
        pool_span = 2**level_id
        pooled_cols = 2 * column_count // pool_span
        for tap_id in range(tap_count):
            centre = (positions + column_count // 2) // pool_span + tap_id - radius_len
            inside = (centre >= 0) & (centre < pooled_cols)
            for inner_id in range(pool_span):
                lookup[
                    positions[inside],
                    centre[inside] * pool_span + inner_id,
                    level_id * tap_count + tap_id,
                ] = (
                    1.0 / pool_span
                )
    return lookup


def tap_stack(padded, extent, axis_dim, kernel_len):
    return jnp.concatenate(
        [
            lax.slice_in_dim(padded, tap_id, tap_id + extent, axis=axis_dim)
            for tap_id in range(kernel_len)
        ],
        axis=-1,
    )


def conv_apply(padded, weight_taps, extent, axis_dim):
    kernel_len, in_chan, out_chan = weight_taps.shape
    stacked = tap_stack(padded, extent, axis_dim, kernel_len)
    flat_taps = stacked.reshape(-1, kernel_len * in_chan)
    result = jnp.dot(
        flat_taps,
        weight_taps.reshape(kernel_len * in_chan, out_chan),
        preferred_element_type=jnp.float32,
    )
    return result.reshape(stacked.shape[:-1] + (out_chan,))


def conv_weight_grad(padded, deltas, axis_dim):
    extent = deltas.shape[axis_dim]
    kernel_len = padded.shape[axis_dim] - extent + 1
    stacked = tap_stack(padded, extent, axis_dim, kernel_len)
    flat_taps = stacked.reshape(-1, stacked.shape[-1])
    flat_deltas = deltas.reshape(-1, deltas.shape[-1])
    result = lax.dot_general(
        flat_taps, flat_deltas, (((0,), (0,)), ((), ())), preferred_element_type=jnp.float32
    )
    return result.reshape(kernel_len, padded.shape[-1], deltas.shape[-1])


def conv_input_grad(deltas, weight_taps, axis_dim):
    kernel_len, in_chan, out_chan = weight_taps.shape
    backward_taps = lax.dot_general(
        deltas.reshape(-1, out_chan),
        weight_taps.reshape(kernel_len * in_chan, out_chan),
        (((1,), (1,)), ((), ())),
        preferred_element_type=jnp.float32,
    )
    backward_taps = backward_taps.reshape(deltas.shape[:-1] + (kernel_len * in_chan,))
    summed = None
    for tap_id in range(kernel_len):
        tap_part = backward_taps[..., tap_id * in_chan : (tap_id + 1) * in_chan]
        widths = [(0, 0)] * deltas.ndim
        widths[axis_dim] = (tap_id, kernel_len - 1 - tap_id)
        shifted = jnp.pad(tap_part, widths)
        summed = shifted if summed is None else summed + shifted
    return summed


def pad_along(values, axis_dim):
    widths = [(0, 0)] * values.ndim
    widths[axis_dim] = (2, 2)
    return jnp.pad(values, widths)


def crop_along(values, axis_dim):
    extent = values.shape[axis_dim] - 4
    return lax.slice_in_dim(values, 2, extent + 2, axis=axis_dim)


def section_forward(padded, context_parts, weights, axis_dim, extend):
    extent = padded.shape[axis_dim] - 4
    hidden_width = weights.shape[-1]
    own_inputs = lax.slice_in_dim(padded, 2, extent + 2, axis=axis_dim)
    hidden_own = own_inputs[..., :hidden_width].astype(jnp.float32)
    feat_padded = padded[..., hidden_width:]
    update_gate = jax.nn.sigmoid(
        conv_apply(padded, weights[0], extent, axis_dim) + context_parts[0].astype(jnp.float32)
    )
    reset_gate = jax.nn.sigmoid(
        conv_apply(padded, weights[1], extent, axis_dim) + context_parts[1].astype(jnp.float32)
    )
    reset_hidden = (reset_gate * hidden_own).astype(jnp.bfloat16)
    gated_padded = jnp.concatenate([extend(reset_hidden), feat_padded], axis=-1)
    candidate = jnp.tanh(
        conv_apply(gated_padded, weights[2], extent, axis_dim)
        + context_parts[2].astype(jnp.float32)
    )
    blended = (1.0 - update_gate) * hidden_own + update_gate * candidate
    return (blended, (update_gate, reset_gate, candidate, hidden_own, padded, gated_padded))


def section_backward(cotangent, stored, weights, axis_dim, fold_rims):
    update_gate, reset_gate, candidate, hidden_own, padded, gated_padded = stored
    hidden_width = weights.shape[-1]
    delta_cand = (cotangent * update_gate * (1.0 - candidate * candidate)).astype(jnp.bfloat16)
    grad_cand = conv_weight_grad(gated_padded, delta_cand, axis_dim)
    back_gated = fold_rims(conv_input_grad(delta_cand, weights[2][:, :hidden_width], axis_dim))
    delta_update = (
        cotangent * (candidate - hidden_own) * update_gate * (1.0 - update_gate)
    ).astype(jnp.bfloat16)
    delta_reset = (back_gated * hidden_own * reset_gate * (1.0 - reset_gate)).astype(jnp.bfloat16)
    grad_update = conv_weight_grad(padded, delta_update, axis_dim)
    grad_reset = conv_weight_grad(padded, delta_reset, axis_dim)
    grad_stack = jnp.stack([grad_update, grad_reset, grad_cand])
    back_inputs = conv_input_grad(
        delta_update, weights[0][:, :hidden_width], axis_dim
    ) + conv_input_grad(delta_reset, weights[1][:, :hidden_width], axis_dim)
    hidden_back = cotangent * (1.0 - update_gate) + back_gated * reset_gate + fold_rims(back_inputs)
    return (grad_stack, hidden_back)


def extend_gated(values):
    return with_halo(values, (("blk", 1),), 2)


def stripe_rims(values):
    extent = values.shape[1] - 4
    edge_terms = jnp.concatenate([values[:, :2], values[:, extent + 2 :]], axis=1)
    arrived = with_halo(edge_terms, (("blk", 1),), 2)
    own_terms = values[:, 2 : extent + 2]
    from_left = jnp.pad(arrived[:, :2], ((0, 0), (0, extent - 2), (0, 0)))
    from_right = jnp.pad(arrived[:, 6:], ((0, 0), (extent - 2, 0), (0, 0)))
    return own_terms + from_left + from_right


MESH = pl.DeviceIdType.MESH
BAND_CHUNKS = 4


def band_kernel(count, block_ref, band_ref, send_sem, recv_sem):
    me = lax.axis_index("blk")
    odd = lax.rem(me, 2)
    mate = me + 1 - 2 * odd
    has_next = me + 2 < count
    has_prev = me >= 2
    has_far = me >= 4
    rows = block_ref.shape[0] // BAND_CHUNKS

    barrier = pltpu.get_barrier_semaphore()
    pl.semaphore_signal(barrier, inc=1, device_id={"blk": mate}, device_id_type=MESH)

    @pl.when(has_next)
    def _():
        pl.semaphore_signal(barrier, inc=1, device_id={"blk": me + 2}, device_id_type=MESH)

    @pl.when(has_prev)
    def _():
        pl.semaphore_signal(barrier, inc=1, device_id={"blk": me - 2}, device_id_type=MESH)

    pl.semaphore_wait(barrier, 1 + has_next.astype(jnp.int32) + has_prev.astype(jnp.int32))

    def copy(source, kind, slot, chunk, target):
        part = pl.ds(chunk * rows, rows)
        src = block_ref if source is None else band_ref.at[source]
        return pltpu.make_async_remote_copy(
            src_ref=src.at[part],
            dst_ref=band_ref.at[slot, part],
            send_sem=send_sem.at[kind, chunk],
            recv_sem=recv_sem.at[slot, chunk],
            device_id={"blk": target},
            device_id_type=MESH,
        )

    def onward(chunk):
        return copy(None, 0, 1, chunk, me + 2)

    def further(chunk):
        return copy(1, 1, 3, chunk, me + 2)

    chunks = range(BAND_CHUNKS)
    for c in chunks:
        pl.when(has_next)(lambda c=c: onward(c).start())
        pl.when(odd == 0)(lambda c=c: copy(None, 2, 0, c, mate).start())
    for c in chunks:

        @pl.when(has_prev)
        def _(c=c):
            onward(c).wait_recv()
            pl.when(has_next)(lambda: further(c).start())
            pl.when(odd == 0)(lambda: copy(1, 3, 2, c, mate).start())
            pl.when(odd == 1)(lambda: copy(1, 2, 0, c, mate).start())

    for c in chunks:

        @pl.when(has_far)
        def _(c=c):
            further(c).wait_recv()
            pl.when(odd == 1)(lambda: copy(3, 3, 2, c, mate).start())

    near_in = (odd == 1) | has_prev
    third_in = ((odd == 1) & has_prev) | ((odd == 0) & has_far)
    near_out = (odd == 0) | has_prev
    third_out = ((odd == 0) & has_prev) | ((odd == 1) & has_far)
    for c in chunks:
        pl.when(near_in)(lambda c=c: copy(None, 2, 0, c, mate).wait_recv())
        pl.when(third_in)(lambda c=c: copy(1, 3, 2, c, mate).wait_recv())
        pl.when(has_next)(lambda c=c: onward(c).wait_send())
        pl.when(has_next & has_prev)(lambda c=c: further(c).wait_send())
        pl.when(near_out)(lambda c=c: copy(None, 2, 0, c, mate).wait_send())
        pl.when(third_out)(lambda c=c: copy(1, 3, 2, c, mate).wait_send())


def band_exchange(block, count):
    return pl.pallas_call(
        functools.partial(band_kernel, count),
        out_shape=jax.ShapeDtypeStruct((4,) + block.shape, block.dtype),
        in_specs=[pl.BlockSpec(memory_space=pl.ANY)],
        out_specs=pl.BlockSpec(memory_space=pl.ANY),
        scratch_shapes=[
            pltpu.SemaphoreType.DMA((4, BAND_CHUNKS)),
            pltpu.SemaphoreType.DMA((4, BAND_CHUNKS)),
        ],
        compiler_params=pltpu.CompilerParams(collective_id=0, has_side_effects=True),
        name="band_exchange",
    )(block)


def sum_steps(pairs, blks):
    steps = []
    for axis, size in (("pair", pairs), ("blk", blks)):
        mask = 1
        while mask < size:
            steps.append((axis, mask))
            mask *= 2
    return steps


def sum_kernel(steps, g_ref, out_ref, acc, sbuf, rbuf, send_sem, recv_sem):
    places = {axis: lax.axis_index(axis) for axis, _ in steps}
    barrier = pltpu.get_barrier_semaphore()
    partners = []
    bits = []
    for axis, mask in steps:
        place = places[axis]
        bit = lax.rem(place // mask, 2)
        bits.append(bit)
        partners.append({axis: place + mask * (1 - 2 * bit)})
        pl.semaphore_signal(barrier, inc=1, device_id=partners[-1], device_id_type=MESH)
    pl.semaphore_wait(barrier, len(steps))
    total = g_ref.shape[0]
    start = 0
    length = total
    landed = 0
    starts = []
    source = g_ref
    for k in range(len(steps)):
        half = length // 2
        keep = pl.multiple_of(start + bits[k] * half, 16)
        away = pl.multiple_of(start + (1 - bits[k]) * half, 16)
        sbuf[pl.ds(away, half)] = source[pl.ds(away, half)].astype(jnp.bfloat16)
        copy = pltpu.make_async_remote_copy(
            src_ref=sbuf.at[pl.ds(away, half)],
            dst_ref=rbuf.at[pl.ds(landed, half)],
            send_sem=send_sem.at[0, k],
            recv_sem=recv_sem.at[0, k],
            device_id=partners[k],
            device_id_type=MESH,
        )
        copy.start()
        copy.wait()
        acc[pl.ds(keep, half)] = source[pl.ds(keep, half)] + rbuf[pl.ds(landed, half)].astype(jnp.float32)
        source = acc
        starts.append(start)
        landed += half
        start = keep
        length = half
    out_ref[pl.ds(start, length)] = acc[pl.ds(start, length)].astype(jnp.bfloat16)
    for k in reversed(range(len(steps))):
        copy = pltpu.make_async_remote_copy(
            src_ref=out_ref.at[pl.ds(start, length)],
            dst_ref=out_ref.at[pl.ds(start, length)],
            send_sem=send_sem.at[1, k],
            recv_sem=recv_sem.at[1, k],
            device_id=partners[k],
            device_id_type=MESH,
        )
        copy.start()
        copy.wait()
        start = starts[k]
        if k:
            start = pl.multiple_of(start, 16)
        length *= 2


def all_sum(rows, pairs, blks):
    steps = sum_steps(pairs, blks)
    return pl.pallas_call(
        functools.partial(sum_kernel, steps),
        out_shape=jax.ShapeDtypeStruct(rows.shape, jnp.bfloat16),
        in_specs=[pl.BlockSpec(memory_space=pltpu.VMEM)],
        out_specs=pl.BlockSpec(memory_space=pltpu.VMEM),
        scratch_shapes=[
            pltpu.VMEM(rows.shape, jnp.float32),
            pltpu.VMEM(rows.shape, jnp.bfloat16),
            pltpu.VMEM(rows.shape, jnp.bfloat16),
            pltpu.SemaphoreType.DMA((2, len(steps))),
            pltpu.SemaphoreType.DMA((2, len(steps))),
        ],
        compiler_params=pltpu.CompilerParams(
            collective_id=1, has_side_effects=True, vmem_limit_bytes=32 * 1024 * 1024
        ),
        name="all_sum",
    )(rows)


def sum_rows_count(used, devices):
    step = devices * 16
    return -(-used // step) * step


def on_device(left_feats, right_feats, offsets, hidden, context, gru_weights, hidden_grad):
    left_block = left_feats[0]
    right_block = right_feats[0]
    offset = offsets[0]
    stripe = lax.axis_index("blk")
    column_count = left_block.shape[1]
    empty_block = jnp.zeros_like(right_block)
    low_id = stripe - offset - 1
    high_id = stripe - offset
    band = band_exchange(right_block, lax.axis_size("blk"))

    def pick_one(block_id):
        distance = jnp.clip(stripe - block_id, 0, 4)
        picked = lax.dynamic_index_in_dim(band, jnp.maximum(distance - 1, 0), 0, keepdims=False)
        picked = jnp.where(distance == 0, right_block, picked)
        return jnp.where(block_id >= 0, picked, empty_block)

    low_block = pick_one(low_id)
    high_block = pick_one(high_id)
    window = jnp.concatenate([low_block, high_block], axis=1)
    scores = jnp.einsum("hxc,hjc->hxj", left_block, window, preferred_element_type=jnp.float32) * (
        1.0 / math.sqrt(left_block.shape[-1])
    )
    lookup = jnp.asarray(lookup_table(column_count, LEVELS, RADIUS))
    features = jnp.einsum("hxj,xjf->hxf", scores, lookup, precision=lax.Precision.HIGHEST).astype(
        jnp.bfloat16
    )
    context_parts = context[0]
    first_inputs = jnp.concatenate([hidden[0], features], axis=-1)
    first_padded = with_halo(first_inputs, (("blk", 1),), 2)
    first_new, first_stored = section_forward(
        first_padded, context_parts, gru_weights[0], 1, extend_gated
    )
    first_hidden = first_new.astype(jnp.bfloat16)
    second_inputs = jnp.concatenate([first_hidden, features], axis=-1)
    second_new, second_stored = section_forward(
        pad_along(second_inputs, 0),
        context_parts,
        gru_weights[1],
        0,
        functools.partial(pad_along, axis_dim=0),
    )
    second_grads, first_back = section_backward(
        hidden_grad[0], second_stored, gru_weights[1], 0, functools.partial(crop_along, axis_dim=0)
    )
    first_grads, hidden_back = section_backward(
        first_back, first_stored, gru_weights[0], 1, stripe_rims
    )
    pairs, blks = lax.axis_size("pair"), lax.axis_size("blk")
    grads = jnp.stack([first_grads, second_grads])
    shape = grads.shape
    padded_rows = -(-shape[3] // 8) * 8
    grads = jnp.pad(grads, ((0, 0),) * 3 + ((0, padded_rows - shape[3]), (0, 0)))
    rows = grads.reshape(-1, shape[4])
    used = rows.shape[0]
    rows = jnp.pad(rows, ((0, sum_rows_count(used, pairs * blks) - used), (0, 0)))
    summed = all_sum(rows, pairs, blks)[:used].reshape(shape[:3] + (padded_rows, shape[4]))
    grad_stack = summed[:, :, :, : shape[3]].astype(jnp.float32)
    return (second_new.astype(jnp.bfloat16)[None], grad_stack, hidden_back[None])


def solution(mesh):
    placed = (
        P("pair", None, "blk", None),
        P("pair", None, "blk", None),
        P("blk"),
        P("pair", None, "blk", None),
        P("pair", None, None, "blk", None),
        P(),
        P("pair", None, "blk", None),
    )
    return jax.shard_map(
        on_device,
        mesh=mesh,
        in_specs=placed,
        out_specs=(P("pair", None, "blk", None), P(), P("pair", None, "blk", None)),
        check_vma=False,
    )
```

```python
import functools
import math

import jax
import jax.numpy as jnp
import numpy as np
from jax import lax
from jax.experimental import pallas as pl
from jax.experimental.pallas import tpu as pltpu
from jax.sharding import PartitionSpec as P

LEVELS = 4
RADIUS = 4


def lookup_table(column_count, level_count, radius_len):
    tap_count = 2 * radius_len + 1
    lookup = np.zeros((column_count, 2 * column_count, level_count * tap_count), np.float32)
    positions = np.arange(column_count)
    for level_id in range(level_count):
        pool_span = 2**level_id
        pooled_cols = 2 * column_count // pool_span
        for tap_id in range(tap_count):
            centre = (positions + column_count // 2) // pool_span + tap_id - radius_len
            inside = (centre >= 0) & (centre < pooled_cols)
            for inner_id in range(pool_span):
                lookup[
                    positions[inside],
                    centre[inside] * pool_span + inner_id,
                    level_id * tap_count + tap_id,
                ] = (
                    1.0 / pool_span
                )
    return lookup


MESH = pl.DeviceIdType.MESH
BAND_CHUNKS = 4


def band_kernel(count, block_ref, band_ref, send_sem, recv_sem):
    me = lax.axis_index("blk")
    odd = lax.rem(me, 2)
    mate = me + 1 - 2 * odd
    has_next = me + 2 < count
    has_prev = me >= 2
    has_far = me >= 4
    rows = block_ref.shape[0] // BAND_CHUNKS

    barrier = pltpu.get_barrier_semaphore()
    pl.semaphore_signal(barrier, inc=1, device_id={"blk": mate}, device_id_type=MESH)

    @pl.when(has_next)
    def _():
        pl.semaphore_signal(barrier, inc=1, device_id={"blk": me + 2}, device_id_type=MESH)

    @pl.when(has_prev)
    def _():
        pl.semaphore_signal(barrier, inc=1, device_id={"blk": me - 2}, device_id_type=MESH)

    pl.semaphore_wait(barrier, 1 + has_next.astype(jnp.int32) + has_prev.astype(jnp.int32))

    def copy(source, kind, slot, chunk, target):
        part = pl.ds(chunk * rows, rows)
        src = block_ref if source is None else band_ref.at[source]
        return pltpu.make_async_remote_copy(
            src_ref=src.at[part],
            dst_ref=band_ref.at[slot, part],
            send_sem=send_sem.at[kind, chunk],
            recv_sem=recv_sem.at[slot, chunk],
            device_id={"blk": target},
            device_id_type=MESH,
        )

    def onward(chunk):
        return copy(None, 0, 1, chunk, me + 2)

    def further(chunk):
        return copy(1, 1, 3, chunk, me + 2)

    chunks = range(BAND_CHUNKS)
    for c in chunks:
        pl.when(has_next)(lambda c=c: onward(c).start())
        pl.when(odd == 0)(lambda c=c: copy(None, 2, 0, c, mate).start())
    for c in chunks:

        @pl.when(has_prev)
        def _(c=c):
            onward(c).wait_recv()
            pl.when(has_next)(lambda: further(c).start())
            pl.when(odd == 0)(lambda: copy(1, 3, 2, c, mate).start())
            pl.when(odd == 1)(lambda: copy(1, 2, 0, c, mate).start())

    for c in chunks:

        @pl.when(has_far)
        def _(c=c):
            further(c).wait_recv()
            pl.when(odd == 1)(lambda: copy(3, 3, 2, c, mate).start())

    near_in = (odd == 1) | has_prev
    third_in = ((odd == 1) & has_prev) | ((odd == 0) & has_far)
    near_out = (odd == 0) | has_prev
    third_out = ((odd == 0) & has_prev) | ((odd == 1) & has_far)
    for c in chunks:
        pl.when(near_in)(lambda c=c: copy(None, 2, 0, c, mate).wait_recv())
        pl.when(third_in)(lambda c=c: copy(1, 3, 2, c, mate).wait_recv())
        pl.when(has_next)(lambda c=c: onward(c).wait_send())
        pl.when(has_next & has_prev)(lambda c=c: further(c).wait_send())
        pl.when(near_out)(lambda c=c: copy(None, 2, 0, c, mate).wait_send())
        pl.when(third_out)(lambda c=c: copy(1, 3, 2, c, mate).wait_send())


def band_exchange(block, count):
    return pl.pallas_call(
        functools.partial(band_kernel, count),
        out_shape=jax.ShapeDtypeStruct((4,) + block.shape, block.dtype),
        in_specs=[pl.BlockSpec(memory_space=pl.ANY)],
        out_specs=pl.BlockSpec(memory_space=pl.ANY),
        scratch_shapes=[
            pltpu.SemaphoreType.DMA((4, BAND_CHUNKS)),
            pltpu.SemaphoreType.DMA((4, BAND_CHUNKS)),
        ],
        compiler_params=pltpu.CompilerParams(collective_id=0, has_side_effects=True),
        name="band_exchange",
    )(block)


def sum_steps(pairs, blks):
    steps = []
    for axis, size in (("pair", pairs), ("blk", blks)):
        mask = 1
        while mask < size:
            steps.append((axis, mask))
            mask *= 2
    return steps


def sum_kernel(steps, g_ref, out_ref, acc, sbuf, rbuf, send_sem, recv_sem):
    places = {axis: lax.axis_index(axis) for axis, _ in steps}
    barrier = pltpu.get_barrier_semaphore()
    partners = []
    bits = []
    for axis, mask in steps:
        place = places[axis]
        bit = lax.rem(place // mask, 2)
        bits.append(bit)
        partners.append({axis: place + mask * (1 - 2 * bit)})
        pl.semaphore_signal(barrier, inc=1, device_id=partners[-1], device_id_type=MESH)
    pl.semaphore_wait(barrier, len(steps))
    total = g_ref.shape[0]
    start = 0
    length = total
    landed = 0
    starts = []
    source = g_ref
    for k in range(len(steps)):
        half = length // 2
        keep = pl.multiple_of(start + bits[k] * half, 16)
        away = pl.multiple_of(start + (1 - bits[k]) * half, 16)
        sbuf[pl.ds(away, half)] = source[pl.ds(away, half)].astype(jnp.bfloat16)
        copy = pltpu.make_async_remote_copy(
            src_ref=sbuf.at[pl.ds(away, half)],
            dst_ref=rbuf.at[pl.ds(landed, half)],
            send_sem=send_sem.at[0, k],
            recv_sem=recv_sem.at[0, k],
            device_id=partners[k],
            device_id_type=MESH,
        )
        copy.start()
        copy.wait()
        acc[pl.ds(keep, half)] = source[pl.ds(keep, half)] + rbuf[pl.ds(landed, half)].astype(jnp.float32)
        source = acc
        starts.append(start)
        landed += half
        start = keep
        length = half
    out_ref[pl.ds(start, length)] = acc[pl.ds(start, length)].astype(jnp.bfloat16)
    for k in reversed(range(len(steps))):
        copy = pltpu.make_async_remote_copy(
            src_ref=out_ref.at[pl.ds(start, length)],
            dst_ref=out_ref.at[pl.ds(start, length)],
            send_sem=send_sem.at[1, k],
            recv_sem=recv_sem.at[1, k],
            device_id=partners[k],
            device_id_type=MESH,
        )
        copy.start()
        copy.wait()
        start = starts[k]
        if k:
            start = pl.multiple_of(start, 16)
        length *= 2


def all_sum(rows, pairs, blks):
    steps = sum_steps(pairs, blks)
    return pl.pallas_call(
        functools.partial(sum_kernel, steps),
        out_shape=jax.ShapeDtypeStruct(rows.shape, jnp.bfloat16),
        in_specs=[pl.BlockSpec(memory_space=pltpu.VMEM)],
        out_specs=pl.BlockSpec(memory_space=pltpu.VMEM),
        scratch_shapes=[
            pltpu.VMEM(rows.shape, jnp.float32),
            pltpu.VMEM(rows.shape, jnp.bfloat16),
            pltpu.VMEM(rows.shape, jnp.bfloat16),
            pltpu.SemaphoreType.DMA((2, len(steps))),
            pltpu.SemaphoreType.DMA((2, len(steps))),
        ],
        compiler_params=pltpu.CompilerParams(
            collective_id=1, has_side_effects=True, vmem_limit_bytes=32 * 1024 * 1024
        ),
        name="all_sum",
    )(rows)


def sum_rows_count(used, devices):
    step = devices * 16
    return -(-used // step) * step


NT = (((1,), (1,)), ((), ()))


def flat(values):
    return values.reshape(-1, values.shape[-1])


def core_kernel(
    count,
    piece,
    left_ref,
    window_ref,
    table_ref,
    hidden_ref,
    context_ref,
    weights_ref,
    grad_ref,
    new_ref,
    hidden_back_ref,
    g_ref,
    corr,
    x0,
    x1,
    rx0,
    rx1,
    dq0,
    dq1,
    dzr0,
    dzr1,
    ctx0,
    z0,
    r0,
    q0,
    z1,
    r1,
    g0,
    acc,
    send_sem,
    recv_sem,
):
    height, width, hd = hidden_ref.shape
    taps = weights_ref.shape[2]
    me = lax.axis_index("blk")
    has_left = me >= 1
    has_right = me + 1 < count
    bf16, f32 = jnp.bfloat16, jnp.float32
    part = 16

    for ref in (x0, x1, rx0, rx1, dq0, dq1, dzr0, dzr1):
        edge = jnp.zeros((2,) + ref.shape[1:], bf16)
        ref[pl.ds(0, 2)] = edge
        ref[pl.ds(ref.shape[0] - 2, 2)] = edge

    barrier = pltpu.get_barrier_semaphore()

    @pl.when(has_left)
    def _():
        pl.semaphore_signal(barrier, inc=1, device_id={"blk": me - 1}, device_id_type=MESH)

    @pl.when(has_right)
    def _():
        pl.semaphore_signal(barrier, inc=1, device_id={"blk": me + 1}, device_id_type=MESH)

    pl.semaphore_wait(barrier, has_left.astype(jnp.int32) + has_right.astype(jnp.int32))

    def edges(ref, number):
        to_left = pltpu.make_async_remote_copy(
            src_ref=ref.at[pl.ds(2, 2)],
            dst_ref=ref.at[pl.ds(width + 2, 2)],
            send_sem=send_sem.at[number, 0],
            recv_sem=recv_sem.at[number, 0],
            device_id={"blk": me - 1},
            device_id_type=MESH,
        )
        to_right = pltpu.make_async_remote_copy(
            src_ref=ref.at[pl.ds(width, 2)],
            dst_ref=ref.at[pl.ds(0, 2)],
            send_sem=send_sem.at[number, 1],
            recv_sem=recv_sem.at[number, 1],
            device_id={"blk": me + 1},
            device_id_type=MESH,
        )
        return to_left, to_right

    def send_edges(ref, number):
        to_left, to_right = edges(ref, number)
        pl.when(has_left)(lambda: to_left.start())
        pl.when(has_right)(lambda: to_right.start())

    def wait_edges(ref, number):
        to_left, to_right = edges(ref, number)
        pl.when(has_left)(lambda: to_left.wait_send())
        pl.when(has_right)(lambda: to_right.wait_send())
        pl.when(has_right)(lambda: to_left.wait_recv())
        pl.when(has_left)(lambda: to_right.wait_recv())

    @pl.loop(0, height // part)
    def _(c):
        rows = pl.ds(pl.multiple_of(c * part, part), part)
        x0[pl.ds(2, width), rows, pl.ds(0, hd)] = jnp.swapaxes(
            hidden_ref[rows].astype(f32), 0, 1
        ).astype(bf16)
        for gate in range(3):
            ctx0[gate, :, rows] = jnp.swapaxes(context_ref[gate, rows].astype(f32), 0, 1)
        scores = jnp.einsum("hxc,hjc->hxj", left_ref[rows], window_ref[rows], preferred_element_type=f32)
        scores = jnp.swapaxes(scores, 0, 1)
        high = scores.astype(bf16).astype(f32)
        corr[:, rows] = jnp.concatenate([high, scores - high], axis=-1)

    @pl.loop(0, width // part)
    def _(c):
        cols = pl.ds(pl.multiple_of(c * part, part), part)
        feats = jnp.einsum(
            "xhj,xjf->xhf", corr[cols].astype(bf16), table_ref[cols], preferred_element_type=f32
        )
        x0[pl.ds(2 + c * part, part), :, pl.ds(hd, hd)] = feats.astype(bf16)
        x1[pl.ds(2, height), cols, pl.ds(hd, hd)] = jnp.swapaxes(feats, 0, 1).astype(bf16)

    send_edges(x0, 0)
    wait_edges(x0, 0)

    def gates(section, x, rx, z, r, context, c):
        total = None
        for k in range(taps):
            w = jnp.concatenate([weights_ref[section, 0, k], weights_ref[section, 1, k]], axis=1)
            term = jnp.dot(flat(x[pl.ds(c * part + k, part)]), w, preferred_element_type=f32)
            total = term if total is None else total + term
        shape = (part,) + x.shape[1:2] + (hd,)
        here = pl.ds(c * part, part)
        z[here] = jax.nn.sigmoid(total[:, :hd].reshape(shape) + context(0, here))
        reset = jax.nn.sigmoid(total[:, hd:].reshape(shape) + context(1, here))
        r[here] = reset
        own = x[pl.ds(c * part + 2, part), :, pl.ds(0, hd)].astype(f32)
        rx[pl.ds(c * part + 2, part)] = (reset * own).astype(bf16)

    def gated(x, rx, first):
        there = pl.ds(first, part)
        return jnp.concatenate([flat(rx[there]), flat(x[there, :, pl.ds(hd, hd)])], axis=1)

    def candidate(section, x, rx, context, c):
        total = None
        for k in range(taps):
            term = jnp.dot(
                gated(x, rx, c * part + k), weights_ref[section, 2, k], preferred_element_type=f32
            )
            total = term if total is None else total + term
        shape = (part,) + x.shape[1:2] + (hd,)
        return jnp.tanh(total.reshape(shape) + context(2, pl.ds(c * part, part)))

    def context_h(gate, here):
        return ctx0[gate, here]

    def context_v(gate, here):
        return context_ref[gate, here].astype(f32)

    @pl.loop(0, width // part)
    def _(c):
        gates(0, x0, rx0, z0, r0, context_h, c)

    send_edges(rx0, 1)
    wait_edges(rx0, 1)

    @pl.loop(0, width // part)
    def _(c):
        here = pl.ds(c * part, part)
        q = candidate(0, x0, rx0, context_h, c)
        q0[here] = q
        z = z0[here]
        own = x0[pl.ds(c * part + 2, part), :, pl.ds(0, hd)].astype(f32)
        blended = (1.0 - z) * own + z * q
        cols = pl.ds(pl.multiple_of(c * part, part), part)
        x1[pl.ds(2, height), cols, pl.ds(0, hd)] = jnp.swapaxes(blended, 0, 1).astype(bf16)

    @pl.loop(0, height // part)
    def _(c):
        gates(1, x1, rx1, z1, r1, context_v, c)

    def deltas(g, z, q, own, dq, dzr, inner):
        dq[inner] = (g * z * (1.0 - q * q)).astype(bf16)
        dzr[inner, :, pl.ds(0, hd)] = (g * (q - own) * z * (1.0 - z)).astype(bf16)

    @pl.loop(0, height // part)
    def _(c):
        here = pl.ds(c * part, part)
        inner = pl.ds(c * part + 2, part)
        q = candidate(1, x1, rx1, context_v, c)
        z = z1[here]
        own = x1[inner, :, pl.ds(0, hd)].astype(f32)
        new_ref[here] = ((1.0 - z) * own + z * q).astype(bf16)
        deltas(grad_ref[here], z, q, own, dq1, dzr1, inner)

    def back_reset(section, x, g, z, r, dq, dzr, c):
        here = pl.ds(c * part, part)
        inner = pl.ds(c * part + 2, part)
        total = None
        for k in range(taps):
            term = lax.dot_general(
                flat(dq[pl.ds(c * part + taps - 1 - k, part)]),
                weights_ref[section, 2, k, pl.ds(0, hd)],
                NT,
                preferred_element_type=f32,
            )
            total = term if total is None else total + term
        total = total.reshape((part,) + x.shape[1:2] + (hd,))
        reset = r[here]
        own = x[inner, :, pl.ds(0, hd)].astype(f32)
        dzr[inner, :, pl.ds(hd, hd)] = (total * own * reset * (1.0 - reset)).astype(bf16)
        r[here] = g[here] * (1.0 - z[here]) + total * reset

    def back_hidden(section, r, dzr, c):
        total = None
        for k in range(taps):
            w = jnp.concatenate(
                [
                    weights_ref[section, 0, k, pl.ds(0, hd)],
                    weights_ref[section, 1, k, pl.ds(0, hd)],
                ],
                axis=1,
            )
            term = lax.dot_general(
                flat(dzr[pl.ds(c * part + taps - 1 - k, part)]), w, NT, preferred_element_type=f32
            )
            total = term if total is None else total + term
        total = total.reshape((part,) + dzr.shape[1:2] + (hd,))
        return r[pl.ds(c * part, part)] + total

    def weight_grads_zr(section, x, dzr, blocks):
        acc[...] = jnp.zeros_like(acc)

        @pl.loop(0, blocks)
        def _(c):
            d = flat(dzr[pl.ds(c * part + 2, part)]).astype(f32).T.astype(bf16)
            for k in range(taps):
                acc[k] += jnp.dot(d, flat(x[pl.ds(c * part + k, part)]), preferred_element_type=f32)

        for k in range(taps):
            for gate in range(2):
                place = ((section * 3 + gate) * taps + k) * piece
                g_ref[pl.ds(place, piece)] = acc[k, pl.ds(gate * hd, hd)].T[:piece]

    def weight_grads_q(section, x, rx, dq, blocks):
        half = pl.ds(0, hd)
        acc[:, half] = jnp.zeros((taps, hd, 2 * hd), f32)

        @pl.loop(0, blocks)
        def _(c):
            d = flat(dq[pl.ds(c * part + 2, part)]).astype(f32).T.astype(bf16)
            for k in range(taps):
                acc[k, half] += jnp.dot(d, gated(x, rx, c * part + k), preferred_element_type=f32)

        for k in range(taps):
            place = ((section * 3 + 2) * taps + k) * piece
            g_ref[pl.ds(place, piece)] = acc[k, half].T[:piece]

    @pl.loop(0, height // part)
    def _(c):
        back_reset(1, x1, grad_ref, z1, r1, dq1, dzr1, c)

    @pl.loop(0, height // part)
    def _(c):
        rows = pl.ds(pl.multiple_of(c * part, part), part)
        g0[:, rows] = jnp.swapaxes(back_hidden(1, r1, dzr1, c), 0, 1)

    @pl.loop(0, width // part)
    def _(c):
        here = pl.ds(c * part, part)
        inner = pl.ds(c * part + 2, part)
        own = x0[inner, :, pl.ds(0, hd)].astype(f32)
        deltas(g0[here], z0[here], q0[here], own, dq0, dzr0, inner)

    send_edges(dq0, 2)
    weight_grads_zr(1, x1, dzr1, height // part)
    weight_grads_q(1, x1, rx1, dq1, height // part)
    wait_edges(dq0, 2)

    @pl.loop(0, width // part)
    def _(c):
        back_reset(0, x0, g0, z0, r0, dq0, dzr0, c)

    send_edges(dzr0, 3)
    weight_grads_q(0, x0, rx0, dq0, width // part)
    weight_grads_zr(0, x0, dzr0, width // part)
    wait_edges(dzr0, 3)

    @pl.loop(0, width // part)
    def _(c):
        cols = pl.ds(pl.multiple_of(c * part, part), part)
        hidden_back_ref[:, cols] = jnp.swapaxes(back_hidden(0, r0, dzr0, c), 0, 1)

    used = 2 * 3 * taps * piece
    if used < g_ref.shape[0]:
        g_ref[pl.ds(used, g_ref.shape[0] - used)] = jnp.zeros((g_ref.shape[0] - used, hd), f32)


def core(left, window, table, hidden, context, weights, hidden_grad, count, piece, sum_rows):
    height, width, hd = hidden.shape
    taps = weights.shape[2]
    bf16, f32 = jnp.bfloat16, jnp.float32
    vmem = pl.BlockSpec(memory_space=pltpu.VMEM)
    across = (width, height, hd)
    down = (height, width, hd)

    def padded(shape, wide):
        return pltpu.VMEM((shape[0] + 4, shape[1], wide * hd), bf16)

    return pl.pallas_call(
        functools.partial(core_kernel, count, piece),
        out_shape=(
            jax.ShapeDtypeStruct(hidden.shape, bf16),
            jax.ShapeDtypeStruct(hidden.shape, f32),
            jax.ShapeDtypeStruct((sum_rows, hd), f32),
        ),
        in_specs=[vmem] * 7,
        out_specs=(vmem,) * 3,
        scratch_shapes=[
            pltpu.VMEM((width, height, 4 * width), f32),
            padded(across, 2),
            padded(down, 2),
            padded(across, 1),
            padded(down, 1),
            padded(across, 1),
            padded(down, 1),
            padded(across, 2),
            padded(down, 2),
            pltpu.VMEM((3,) + across, f32),
            pltpu.VMEM(across, f32),
            pltpu.VMEM(across, f32),
            pltpu.VMEM(across, f32),
            pltpu.VMEM(down, f32),
            pltpu.VMEM(down, f32),
            pltpu.VMEM(across, f32),
            pltpu.VMEM((taps, 2 * hd, 2 * hd), f32),
            pltpu.SemaphoreType.DMA((4, 2)),
            pltpu.SemaphoreType.DMA((4, 2)),
        ],
        compiler_params=pltpu.CompilerParams(
            collective_id=2, has_side_effects=True, vmem_limit_bytes=58 * 1024 * 1024
        ),
        name="core",
    )(left, window, table, hidden, context, weights, hidden_grad)


def on_device(left_feats, right_feats, offsets, hidden, context, gru_weights, hidden_grad):
    left_block = left_feats[0]
    right_block = right_feats[0]
    offset = offsets[0]
    stripe = lax.axis_index("blk")
    column_count = left_block.shape[1]
    empty_block = jnp.zeros_like(right_block)
    low_id = stripe - offset - 1
    high_id = stripe - offset
    band = band_exchange(right_block, lax.axis_size("blk"))

    def pick_one(block_id):
        distance = jnp.clip(stripe - block_id, 0, 4)
        picked = lax.dynamic_index_in_dim(band, jnp.maximum(distance - 1, 0), 0, keepdims=False)
        picked = jnp.where(distance == 0, right_block, picked)
        return jnp.where(block_id >= 0, picked, empty_block)

    low_block = pick_one(low_id)
    high_block = pick_one(high_id)
    window = jnp.concatenate([low_block, high_block], axis=1)
    table = lookup_table(column_count, LEVELS, RADIUS) / math.sqrt(left_block.shape[-1])
    hd = gru_weights.shape[-1]
    table = np.concatenate([table, table], axis=1)
    table = np.pad(table, ((0, 0), (0, 0), (0, hd - table.shape[2])))
    table = jnp.asarray(table, jnp.bfloat16)
    pairs, blks = lax.axis_size("pair"), lax.axis_size("blk")
    shape = gru_weights.shape
    piece = -(-shape[3] // 8) * 8
    used = math.prod(shape[:3]) * piece
    weights = jnp.pad(gru_weights, ((0, 0),) * 3 + ((0, 2 * hd - shape[3]), (0, 0)))
    new_hidden, hidden_back, rows = core(
        left_block,
        window,
        table,
        hidden[0],
        context[0],
        weights,
        hidden_grad[0],
        blks,
        piece,
        sum_rows_count(used, pairs * blks),
    )
    summed = all_sum(rows, pairs, blks)[:used].reshape(shape[:3] + (piece, hd))
    grad_stack = summed[:, :, :, : shape[3]].astype(jnp.float32)
    return (new_hidden[None], grad_stack, hidden_back[None])


def solution(mesh):
    placed = (
        P("pair", None, "blk", None),
        P("pair", None, "blk", None),
        P("blk"),
        P("pair", None, "blk", None),
        P("pair", None, None, "blk", None),
        P(),
        P("pair", None, "blk", None),
    )
    return jax.shard_map(
        on_device,
        mesh=mesh,
        in_specs=placed,
        out_specs=(P("pair", None, "blk", None), P(), P("pair", None, "blk", None)),
        check_vma=False,
    )
```

```python
import functools
import math

import jax
import jax.numpy as jnp
import numpy as np
from jax import lax
from jax.experimental import pallas as pl
from jax.experimental.pallas import tpu as pltpu
from jax.sharding import PartitionSpec as P

LEVELS = 4
RADIUS = 4


def lookup_table(column_count, level_count, radius_len):
    tap_count = 2 * radius_len + 1
    lookup = np.zeros((column_count, 2 * column_count, level_count * tap_count), np.float32)
    positions = np.arange(column_count)
    for level_id in range(level_count):
        pool_span = 2**level_id
        pooled_cols = 2 * column_count // pool_span
        for tap_id in range(tap_count):
            centre = (positions + column_count // 2) // pool_span + tap_id - radius_len
            inside = (centre >= 0) & (centre < pooled_cols)
            for inner_id in range(pool_span):
                lookup[
                    positions[inside],
                    centre[inside] * pool_span + inner_id,
                    level_id * tap_count + tap_id,
                ] = (
                    1.0 / pool_span
                )
    return lookup


MESH = pl.DeviceIdType.MESH
BAND_CHUNKS = 8


def sum_steps(pairs, blks):
    steps = []
    for axis, size in (("pair", pairs), ("blk", blks)):
        mask = 1
        while mask < size:
            steps.append((axis, mask))
            mask *= 2
    return steps


def sum_rows_count(used, devices):
    step = devices * 16
    return -(-used // step) * step


NT = (((1,), (1,)), ((), ()))


def flat(values):
    return values.reshape(-1, values.shape[-1])


def core_kernel(
    count,
    piece,
    steps,
    offset_ref,
    block_in,
    left_in,
    table_in,
    hidden_in,
    context_in,
    weights_in,
    grad_in,
    new_ref,
    hidden_back_ref,
    sum_ref,
    band,
    left_ref,
    table_ref,
    hidden_ref,
    context_ref,
    narrow_ref,
    grad_ref,
    weights_ref,
    g_ref,
    sbuf,
    rbuf,
    corr,
    x0,
    x1,
    rx0,
    rx1,
    dq0,
    dq1,
    dzr0,
    dzr1,
    ctx0,
    z0,
    r0,
    q0,
    z1,
    r1,
    g0,
    acc,
    send_sem,
    recv_sem,
    band_send,
    band_recv,
    sum_send,
    sum_recv,
    local_sem,
):
    height, width, hd = hidden_ref.shape
    taps = weights_ref.shape[2]
    me = lax.axis_index("blk")
    has_left = me >= 1
    has_right = me + 1 < count
    bf16, f32 = jnp.bfloat16, jnp.float32
    part = 16

    for ref in (x0, x1, rx0, rx1, dq0, dq1, dzr0, dzr1):
        edge = jnp.zeros((2,) + ref.shape[1:], bf16)
        ref[pl.ds(0, 2)] = edge
        ref[pl.ds(ref.shape[0] - 2, 2)] = edge

    for distance in range(1, 5):

        @pl.when(me < distance)
        def _(distance=distance):
            band[distance] = jnp.zeros(band.shape[1:], bf16)

    barrier = pltpu.get_barrier_semaphore()
    places = {"pair": lax.axis_index("pair"), "blk": me}
    bits = []
    partners = []
    for axis, mask in steps:
        bit = lax.rem(places[axis] // mask, 2)
        bits.append(bit)
        partners.append({axis: places[axis] + mask * (1 - 2 * bit)})
        pl.semaphore_signal(barrier, inc=1, device_id=partners[-1], device_id_type=MESH)
    has_next = me + 2 < count
    has_prev = me >= 2
    has_far = me >= 4
    expected = len(steps)
    for present, shift in ((has_left, -1), (has_right, 1), (has_prev, -2), (has_next, 2)):

        @pl.when(present)
        def _(shift=shift):
            pl.semaphore_signal(barrier, inc=1, device_id={"blk": me + shift}, device_id_type=MESH)

        expected = expected + present.astype(jnp.int32)
    pl.semaphore_wait(barrier, expected)

    odd = lax.rem(me, 2)
    mate = me + 1 - 2 * odd
    band_rows = height // BAND_CHUNKS

    def band_copy(source, kind, slot, chunk, target):
        part = pl.ds(chunk * band_rows, band_rows)
        src = block_in.at[part] if source is None else band.at[source, part]
        return pltpu.make_async_remote_copy(
            src_ref=src,
            dst_ref=band.at[slot, part],
            send_sem=band_send.at[kind, chunk],
            recv_sem=band_recv.at[slot - 1, chunk],
            device_id={"blk": target},
            device_id_type=MESH,
        )

    def onward(chunk):
        return band_copy(None, 0, 2, chunk, me + 2)

    def further(chunk):
        return band_copy(2, 1, 4, chunk, me + 2)

    chunks = range(BAND_CHUNKS)
    for c in chunks:
        pl.when(has_next)(lambda c=c: onward(c).start())
        pl.when(odd == 0)(lambda c=c: band_copy(None, 2, 1, c, mate).start())

    local = [
        pltpu.make_async_copy(src, dst, local_sem.at[i])
        for i, (src, dst) in enumerate(
            (
                (hidden_in, hidden_ref),
                (context_in, context_ref),
                (weights_in, narrow_ref),
                (left_in, left_ref),
                (block_in, band.at[0]),
                (table_in, table_ref),
                (grad_in, grad_ref),
            )
        )
    ]
    for copy in local:
        copy.start()

    def edges(ref, number):
        to_left = pltpu.make_async_remote_copy(
            src_ref=ref.at[pl.ds(2, 2)],
            dst_ref=ref.at[pl.ds(width + 2, 2)],
            send_sem=send_sem.at[number, 0],
            recv_sem=recv_sem.at[number, 0],
            device_id={"blk": me - 1},
            device_id_type=MESH,
        )
        to_right = pltpu.make_async_remote_copy(
            src_ref=ref.at[pl.ds(width, 2)],
            dst_ref=ref.at[pl.ds(0, 2)],
            send_sem=send_sem.at[number, 1],
            recv_sem=recv_sem.at[number, 1],
            device_id={"blk": me + 1},
            device_id_type=MESH,
        )
        return to_left, to_right

    def send_edges(ref, number):
        to_left, to_right = edges(ref, number)
        pl.when(has_left)(lambda: to_left.start())
        pl.when(has_right)(lambda: to_right.start())

    def wait_edges(ref, number):
        to_left, to_right = edges(ref, number)
        pl.when(has_left)(lambda: to_left.wait_send())
        pl.when(has_right)(lambda: to_right.wait_send())
        pl.when(has_right)(lambda: to_left.wait_recv())
        pl.when(has_left)(lambda: to_right.wait_recv())

    for copy in local:
        copy.wait()

    @pl.loop(0, height // part)
    def _(c):
        rows = pl.ds(pl.multiple_of(c * part, part), part)
        x0[pl.ds(2, width), rows, pl.ds(0, hd)] = jnp.swapaxes(
            hidden_ref[rows].astype(f32), 0, 1
        ).astype(bf16)

    for c in chunks:

        @pl.when(has_prev)
        def _(c=c):
            onward(c).wait_recv()
            pl.when(has_next)(lambda: further(c).start())
            pl.when(odd == 0)(lambda: band_copy(2, 3, 3, c, mate).start())
            pl.when(odd == 1)(lambda: band_copy(2, 2, 1, c, mate).start())

    @pl.loop(0, height // part)
    def _(c):
        rows = pl.ds(pl.multiple_of(c * part, part), part)
        for gate in range(3):
            ctx0[gate, :, rows] = jnp.swapaxes(context_ref[gate, rows].astype(f32), 0, 1)

    deep = narrow_ref.shape[3]
    tail = deep // 16 * 16
    for section in range(2):
        for gate in range(3):
            for k in range(taps):
                weights_ref[section, gate, k, pl.ds(0, tail)] = narrow_ref[section, gate, k, pl.ds(0, tail)]
                rest = narrow_ref[section, gate, k, pl.ds(tail, deep - tail)].astype(f32)
                blank = jnp.zeros((2 * hd - deep, hd), f32)
                weights_ref[section, gate, k, pl.ds(tail, 2 * hd - tail)] = jnp.concatenate(
                    [rest, blank], axis=0
                ).astype(bf16)

    for c in chunks:

        @pl.when(has_far)
        def _(c=c):
            further(c).wait_recv()
            pl.when(odd == 1)(lambda: band_copy(4, 3, 3, c, mate).start())

    near_in = (odd == 1) | has_prev
    third_in = ((odd == 1) & has_prev) | ((odd == 0) & has_far)
    near_out = (odd == 0) | has_prev
    third_out = ((odd == 0) & has_prev) | ((odd == 1) & has_far)
    for c in chunks:
        pl.when(near_in)(lambda c=c: band_copy(None, 2, 1, c, mate).wait_recv())
        pl.when(third_in)(lambda c=c: band_copy(2, 3, 3, c, mate).wait_recv())

    offset = offset_ref[0]

    @pl.loop(0, height // part)
    def _(c):
        rows = pl.ds(pl.multiple_of(c * part, part), part)
        window = jnp.concatenate([band[offset + 1, rows], band[offset, rows]], axis=1)
        scores = jnp.einsum("hxc,hjc->hxj", left_ref[rows], window, preferred_element_type=f32)
        scores = jnp.swapaxes(scores, 0, 1)
        high = scores.astype(bf16).astype(f32)
        corr[:, rows] = jnp.concatenate([high, scores - high], axis=-1)

    @pl.loop(0, width // part)
    def _(c):
        cols = pl.ds(pl.multiple_of(c * part, part), part)
        feats = jnp.einsum(
            "xhj,xjf->xhf", corr[cols].astype(bf16), table_ref[cols], preferred_element_type=f32
        )
        x0[pl.ds(2 + c * part, part), :, pl.ds(hd, hd)] = feats.astype(bf16)
        x1[pl.ds(2, height), cols, pl.ds(hd, hd)] = jnp.swapaxes(feats, 0, 1).astype(bf16)

    send_edges(x0, 0)
    wait_edges(x0, 0)

    def gates(section, x, rx, z, r, context, c):
        total = None
        for k in range(taps):
            w = jnp.concatenate([weights_ref[section, 0, k], weights_ref[section, 1, k]], axis=1)
            term = jnp.dot(flat(x[pl.ds(c * part + k, part)]), w, preferred_element_type=f32)
            total = term if total is None else total + term
        shape = (part,) + x.shape[1:2] + (hd,)
        here = pl.ds(c * part, part)
        z[here] = jax.nn.sigmoid(total[:, :hd].reshape(shape) + context(0, here))
        reset = jax.nn.sigmoid(total[:, hd:].reshape(shape) + context(1, here))
        r[here] = reset
        own = x[pl.ds(c * part + 2, part), :, pl.ds(0, hd)].astype(f32)
        rx[pl.ds(c * part + 2, part)] = (reset * own).astype(bf16)

    def gated(x, rx, first):
        there = pl.ds(first, part)
        return jnp.concatenate([flat(rx[there]), flat(x[there, :, pl.ds(hd, hd)])], axis=1)

    def candidate(section, x, rx, context, c):
        total = None
        for k in range(taps):
            term = jnp.dot(
                gated(x, rx, c * part + k), weights_ref[section, 2, k], preferred_element_type=f32
            )
            total = term if total is None else total + term
        shape = (part,) + x.shape[1:2] + (hd,)
        return jnp.tanh(total.reshape(shape) + context(2, pl.ds(c * part, part)))

    def context_h(gate, here):
        return ctx0[gate, here]

    def context_v(gate, here):
        return context_ref[gate, here].astype(f32)

    @pl.loop(0, width // part)
    def _(c):
        gates(0, x0, rx0, z0, r0, context_h, c)

    send_edges(rx0, 1)
    wait_edges(rx0, 1)

    @pl.loop(0, width // part)
    def _(c):
        here = pl.ds(c * part, part)
        q = candidate(0, x0, rx0, context_h, c)
        q0[here] = q
        z = z0[here]
        own = x0[pl.ds(c * part + 2, part), :, pl.ds(0, hd)].astype(f32)
        blended = (1.0 - z) * own + z * q
        cols = pl.ds(pl.multiple_of(c * part, part), part)
        x1[pl.ds(2, height), cols, pl.ds(0, hd)] = jnp.swapaxes(blended, 0, 1).astype(bf16)

    @pl.loop(0, height // part)
    def _(c):
        gates(1, x1, rx1, z1, r1, context_v, c)

    def deltas(g, z, q, own, dq, dzr, inner):
        dq[inner] = (g * z * (1.0 - q * q)).astype(bf16)
        dzr[inner, :, pl.ds(0, hd)] = (g * (q - own) * z * (1.0 - z)).astype(bf16)

    @pl.loop(0, height // part)
    def _(c):
        here = pl.ds(c * part, part)
        inner = pl.ds(c * part + 2, part)
        q = candidate(1, x1, rx1, context_v, c)
        z = z1[here]
        own = x1[inner, :, pl.ds(0, hd)].astype(f32)
        new_ref[here] = ((1.0 - z) * own + z * q).astype(bf16)
        deltas(grad_ref[here], z, q, own, dq1, dzr1, inner)

    def back_reset(section, x, g, z, r, dq, dzr, c):
        here = pl.ds(c * part, part)
        inner = pl.ds(c * part + 2, part)
        total = None
        for k in range(taps):
            term = lax.dot_general(
                flat(dq[pl.ds(c * part + taps - 1 - k, part)]),
                weights_ref[section, 2, k, pl.ds(0, hd)],
                NT,
                preferred_element_type=f32,
            )
            total = term if total is None else total + term
        total = total.reshape((part,) + x.shape[1:2] + (hd,))
        reset = r[here]
        own = x[inner, :, pl.ds(0, hd)].astype(f32)
        dzr[inner, :, pl.ds(hd, hd)] = (total * own * reset * (1.0 - reset)).astype(bf16)
        r[here] = g[here] * (1.0 - z[here]) + total * reset

    def back_hidden(section, r, dzr, c):
        total = None
        for k in range(taps):
            w = jnp.concatenate(
                [
                    weights_ref[section, 0, k, pl.ds(0, hd)],
                    weights_ref[section, 1, k, pl.ds(0, hd)],
                ],
                axis=1,
            )
            term = lax.dot_general(
                flat(dzr[pl.ds(c * part + taps - 1 - k, part)]), w, NT, preferred_element_type=f32
            )
            total = term if total is None else total + term
        total = total.reshape((part,) + dzr.shape[1:2] + (hd,))
        return r[pl.ds(c * part, part)] + total

    def weight_grads_zr(section, x, dzr, blocks):
        acc[...] = jnp.zeros_like(acc)

        @pl.loop(0, blocks)
        def _(c):
            d = flat(dzr[pl.ds(c * part + 2, part)]).astype(f32).T.astype(bf16)
            for k in range(taps):
                acc[k] += jnp.dot(d, flat(x[pl.ds(c * part + k, part)]), preferred_element_type=f32)

        for k in range(taps):
            for gate in range(2):
                place = (gate * taps + k) * piece
                g_ref[section, pl.ds(place, piece)] = acc[k, pl.ds(gate * hd, hd)].T[:piece]

    def weight_grads_q(section, x, rx, dq, blocks):
        half = pl.ds(0, hd)
        acc[:, half] = jnp.zeros((taps, hd, 2 * hd), f32)

        @pl.loop(0, blocks)
        def _(c):
            d = flat(dq[pl.ds(c * part + 2, part)]).astype(f32).T.astype(bf16)
            for k in range(taps):
                acc[k, half] += jnp.dot(d, gated(x, rx, c * part + k), preferred_element_type=f32)

        for k in range(taps):
            place = (2 * taps + k) * piece
            g_ref[section, pl.ds(place, piece)] = acc[k, half].T[:piece]

    @pl.loop(0, height // part)
    def _(c):
        back_reset(1, x1, grad_ref, z1, r1, dq1, dzr1, c)

    @pl.loop(0, height // part)
    def _(c):
        rows = pl.ds(pl.multiple_of(c * part, part), part)
        g0[:, rows] = jnp.swapaxes(back_hidden(1, r1, dzr1, c), 0, 1)

    @pl.loop(0, width // part)
    def _(c):
        here = pl.ds(c * part, part)
        inner = pl.ds(c * part + 2, part)
        own = x0[inner, :, pl.ds(0, hd)].astype(f32)
        deltas(g0[here], z0[here], q0[here], own, dq0, dzr0, inner)

    total_rows = g_ref.shape[1]
    used = 3 * taps * piece
    if used < total_rows:
        for section in range(2):
            g_ref[section, pl.ds(used, total_rows - used)] = jnp.zeros((total_rows - used, hd), f32)

    depth = len(steps)
    spans = [(0, total_rows)]
    for k in range(depth):
        first, length = spans[-1]
        half = length // 2
        spans.append((pl.multiple_of(first + bits[k] * half, 16), half))

    def sum_copy(section, k):
        if k < depth:
            first, length = spans[k]
            half = length // 2
            away = pl.multiple_of(first + (1 - bits[k]) * half, 16)
            src = sbuf.at[section, pl.ds(away, half)]
            dst = rbuf.at[section, pl.ds(total_rows - length, half)]
            step = k
        else:
            step = 2 * depth - 1 - k
            first, length = spans[step + 1]
            src = dst = sum_ref.at[section, pl.ds(first, length)]
        return pltpu.make_async_remote_copy(
            src_ref=src,
            dst_ref=dst,
            send_sem=sum_send.at[section, k],
            recv_sem=sum_recv.at[section, k],
            device_id=partners[step],
            device_id_type=MESH,
        )

    def begin(section, k):
        if k < depth:
            first, length = spans[k]
            half = length // 2
            away = pl.multiple_of(first + (1 - bits[k]) * half, 16)
            sbuf[section, pl.ds(away, half)] = g_ref[section, pl.ds(away, half)].astype(bf16)
        sum_copy(section, k).start()

    def finish(section, k):
        sum_copy(section, k).wait()
        if k < depth:
            keep, half = spans[k + 1]
            here = pl.ds(keep, half)
            landed = rbuf[section, pl.ds(total_rows - 2 * half, half)]
            summed = g_ref[section, here] + landed.astype(f32)
            if k == depth - 1:
                sum_ref[section, here] = summed.astype(bf16)
            else:
                g_ref[section, here] = summed

    def turn(section, k):
        if k >= 0:
            finish(section, k)
        if k + 1 < 2 * depth:
            begin(section, k + 1)

    send_edges(dq0, 2)
    weight_grads_zr(1, x1, dzr1, height // part)
    weight_grads_q(1, x1, rx1, dq1, height // part)
    turn(1, -1)
    wait_edges(dq0, 2)

    @pl.loop(0, width // part)
    def _(c):
        back_reset(0, x0, g0, z0, r0, dq0, dzr0, c)

    send_edges(dzr0, 3)
    turn(1, 0)
    weight_grads_q(0, x0, rx0, dq0, width // part)
    turn(1, 1)
    weight_grads_zr(0, x0, dzr0, width // part)
    turn(0, -1)
    turn(1, 2)
    wait_edges(dzr0, 3)

    @pl.loop(0, width // part)
    def _(c):
        cols = pl.ds(pl.multiple_of(c * part, part), part)
        hidden_back_ref[:, cols] = jnp.swapaxes(back_hidden(0, r0, dzr0, c), 0, 1)

    for k in range(2 * depth):
        if k + 3 < 2 * depth:
            turn(1, k + 3)
        turn(0, k)

    for c in chunks:
        pl.when(has_next)(lambda c=c: onward(c).wait_send())
        pl.when(has_next & has_prev)(lambda c=c: further(c).wait_send())
        pl.when(near_out)(lambda c=c: band_copy(None, 2, 1, c, mate).wait_send())
        pl.when(third_out)(lambda c=c: band_copy(2, 3, 3, c, mate).wait_send())


def core(offset, block, left, table, hidden, context, weights, hidden_grad, pairs, count, piece, sum_rows):
    height, width, hd = hidden.shape
    taps = weights.shape[2]
    bf16, f32 = jnp.bfloat16, jnp.float32
    vmem = pl.BlockSpec(memory_space=pltpu.VMEM)
    anywhere = pl.BlockSpec(memory_space=pl.ANY)
    steps = sum_steps(pairs, count)
    narrow = weights.shape

    def held(values):
        return pltpu.VMEM(values.shape, values.dtype)

    across = (width, height, hd)
    down = (height, width, hd)

    def padded(shape, wide):
        return pltpu.VMEM((shape[0] + 4, shape[1], wide * hd), bf16)

    return pl.pallas_call(
        functools.partial(core_kernel, count, piece, steps),
        out_shape=(
            jax.ShapeDtypeStruct(hidden.shape, bf16),
            jax.ShapeDtypeStruct(hidden.shape, f32),
            jax.ShapeDtypeStruct((2, sum_rows, hd), bf16),
        ),
        in_specs=[pl.BlockSpec(memory_space=pltpu.SMEM)] + [anywhere] * 7,
        out_specs=(vmem,) * 3,
        scratch_shapes=[
            pltpu.VMEM((5,) + block.shape, bf16),
            held(left),
            held(table),
            held(hidden),
            held(context),
            held(weights),
            held(hidden_grad),
            pltpu.VMEM(narrow[:3] + (2 * hd, hd), bf16),
            pltpu.VMEM((2, sum_rows, hd), f32),
            pltpu.VMEM((2, sum_rows, hd), bf16),
            pltpu.VMEM((2, sum_rows, hd), bf16),
            pltpu.VMEM((width, height, 4 * width), f32),
            padded(across, 2),
            padded(down, 2),
            padded(across, 1),
            padded(down, 1),
            padded(across, 1),
            padded(down, 1),
            padded(across, 2),
            padded(down, 2),
            pltpu.VMEM((3,) + across, f32),
            pltpu.VMEM(across, f32),
            pltpu.VMEM(across, f32),
            pltpu.VMEM(across, f32),
            pltpu.VMEM(down, f32),
            pltpu.VMEM(down, f32),
            pltpu.VMEM(across, f32),
            pltpu.VMEM((taps, 2 * hd, 2 * hd), f32),
            pltpu.SemaphoreType.DMA((4, 2)),
            pltpu.SemaphoreType.DMA((4, 2)),
            pltpu.SemaphoreType.DMA((4, BAND_CHUNKS)),
            pltpu.SemaphoreType.DMA((4, BAND_CHUNKS)),
            pltpu.SemaphoreType.DMA((2, 2 * len(steps))),
            pltpu.SemaphoreType.DMA((2, 2 * len(steps))),
            pltpu.SemaphoreType.DMA((7,)),
        ],
        compiler_params=pltpu.CompilerParams(
            collective_id=0, has_side_effects=True, vmem_limit_bytes=58 * 1024 * 1024
        ),
        name="core",
    )(offset, block, left, table, hidden, context, weights, hidden_grad)


def on_device(left_feats, right_feats, offsets, hidden, context, gru_weights, hidden_grad):
    left_block = left_feats[0]
    right_block = right_feats[0]
    column_count = left_block.shape[1]
    table = lookup_table(column_count, LEVELS, RADIUS) / math.sqrt(left_block.shape[-1])
    hd = gru_weights.shape[-1]
    table = np.concatenate([table, table], axis=1)
    table = np.pad(table, ((0, 0), (0, 0), (0, hd - table.shape[2])))
    table = jnp.asarray(table, jnp.bfloat16)
    pairs, blks = lax.axis_size("pair"), lax.axis_size("blk")
    shape = gru_weights.shape
    piece = -(-shape[3] // 8) * 8
    used = math.prod(shape[1:3]) * piece
    new_hidden, hidden_back, summed = core(
        offsets,
        right_block,
        left_block,
        table,
        hidden[0],
        context[0],
        gru_weights,
        hidden_grad[0],
        pairs,
        blks,
        piece,
        sum_rows_count(used, pairs * blks),
    )
    summed = summed[:, :used].reshape(shape[:3] + (piece, hd))
    grad_stack = summed[:, :, :, : shape[3]].astype(jnp.float32)
    return (new_hidden[None], grad_stack, hidden_back[None])


def solution(mesh):
    placed = (
        P("pair", None, "blk", None),
        P("pair", None, "blk", None),
        P("blk"),
        P("pair", None, "blk", None),
        P("pair", None, None, "blk", None),
        P(),
        P("pair", None, "blk", None),
    )
    return jax.shard_map(
        on_device,
        mesh=mesh,
        in_specs=placed,
        out_specs=(P("pair", None, "blk", None), P(), P("pair", None, "blk", None)),
        check_vma=False,
    )
```

```python
import functools
import math

import jax
import jax.numpy as jnp
import numpy as np
from jax import lax
from jax.experimental import pallas as pl
from jax.experimental.pallas import tpu as pltpu
from jax.sharding import PartitionSpec as P

LEVELS = 4
RADIUS = 4


def lookup_table(column_count, level_count, radius_len):
    tap_count = 2 * radius_len + 1
    lookup = np.zeros((column_count, 2 * column_count, level_count * tap_count), np.float32)
    positions = np.arange(column_count)
    for level_id in range(level_count):
        pool_span = 2**level_id
        pooled_cols = 2 * column_count // pool_span
        for tap_id in range(tap_count):
            centre = (positions + column_count // 2) // pool_span + tap_id - radius_len
            inside = (centre >= 0) & (centre < pooled_cols)
            for inner_id in range(pool_span):
                lookup[
                    positions[inside],
                    centre[inside] * pool_span + inner_id,
                    level_id * tap_count + tap_id,
                ] = (
                    1.0 / pool_span
                )
    return lookup


MESH = pl.DeviceIdType.MESH
BAND_CHUNKS = 8


def sum_steps(pairs, blks):
    steps = []
    for axis, size, most in (("pair", pairs, 2), ("blk", blks, 8)):
        stride = 1
        while stride < size:
            members = min(most, size // stride)
            steps.append((axis, stride, members))
            stride *= members
    return steps


def sum_rows_count(used, devices):
    step = devices * 16
    return -(-used // step) * step


NT = (((1,), (1,)), ((), ()))


def flat(values):
    return values.reshape(-1, values.shape[-1])


def core_kernel(
    count,
    piece,
    steps,
    offset_ref,
    block_in,
    left_in,
    table_in,
    hidden_in,
    context_in,
    weights_in,
    grad_in,
    new_ref,
    hidden_back_ref,
    sum_ref,
    band,
    left_ref,
    table_ref,
    hidden_ref,
    context_ref,
    narrow_ref,
    grad_ref,
    weights_ref,
    g_ref,
    sbuf,
    rbuf,
    corr,
    x0,
    x1,
    rx0,
    rx1,
    dq0,
    dq1,
    dzr0,
    dzr1,
    ctx0,
    z0,
    r0,
    q0,
    z1,
    r1,
    g0,
    acc,
    send_sem,
    recv_sem,
    band_send,
    band_recv,
    sum_send,
    sum_recv,
    local_sem,
):
    height, width, hd = hidden_ref.shape
    taps = weights_ref.shape[2]
    me = lax.axis_index("blk")
    has_left = me >= 1
    has_right = me + 1 < count
    bf16, f32 = jnp.bfloat16, jnp.float32
    part = 16

    for ref in (x0, x1, rx0, rx1, dq0, dq1, dzr0, dzr1):
        edge = jnp.zeros((2,) + ref.shape[1:], bf16)
        ref[pl.ds(0, 2)] = edge
        ref[pl.ds(ref.shape[0] - 2, 2)] = edge

    for distance in range(1, 5):

        @pl.when(me < distance)
        def _(distance=distance):
            band[distance] = jnp.zeros(band.shape[1:], bf16)

    barrier = pltpu.get_barrier_semaphore()
    places = {"pair": lax.axis_index("pair"), "blk": me}
    ranks = []
    partners = []
    for axis, stride, members in steps:
        place = places[axis]
        ranks.append(lax.rem(place // stride, members))
        row = [None]
        for d in range(1, members):
            shift = 0
            mask = 1
            while mask < members:
                if d & mask:
                    bit = lax.rem(place // (stride * mask), 2)
                    shift = shift + stride * mask * (1 - 2 * bit)
                mask *= 2
            row.append((place + shift, axis))
            pl.semaphore_signal(barrier, inc=1, device_id={axis: place + shift}, device_id_type=MESH)
        partners.append(row)
    has_next = me + 2 < count
    has_prev = me >= 2
    has_far = me >= 4
    expected = sum(members - 1 for _, _, members in steps)
    for present, shift in ((has_left, -1), (has_right, 1), (has_prev, -2), (has_next, 2)):

        @pl.when(present)
        def _(shift=shift):
            pl.semaphore_signal(barrier, inc=1, device_id={"blk": me + shift}, device_id_type=MESH)

        expected = expected + present.astype(jnp.int32)
    pl.semaphore_wait(barrier, expected)

    odd = lax.rem(me, 2)
    mate = me + 1 - 2 * odd
    band_rows = height // BAND_CHUNKS

    def band_copy(source, kind, slot, chunk, target):
        part = pl.ds(chunk * band_rows, band_rows)
        src = block_in.at[part] if source is None else band.at[source, part]
        return pltpu.make_async_remote_copy(
            src_ref=src,
            dst_ref=band.at[slot, part],
            send_sem=band_send.at[kind, chunk],
            recv_sem=band_recv.at[slot - 1, chunk],
            device_id={"blk": target},
            device_id_type=MESH,
        )

    def onward(chunk):
        return band_copy(None, 0, 2, chunk, me + 2)

    def further(chunk):
        return band_copy(2, 1, 4, chunk, me + 2)

    chunks = range(BAND_CHUNKS)
    for c in chunks:
        pl.when(has_next)(lambda c=c: onward(c).start())
        pl.when(odd == 0)(lambda c=c: band_copy(None, 2, 1, c, mate).start())

    local = [
        pltpu.make_async_copy(src, dst, local_sem.at[i])
        for i, (src, dst) in enumerate(
            (
                (hidden_in, hidden_ref),
                (context_in, context_ref),
                (weights_in, narrow_ref),
                (left_in, left_ref),
                (block_in, band.at[0]),
                (table_in, table_ref),
                (grad_in, grad_ref),
            )
        )
    ]
    for copy in local:
        copy.start()

    def edges(ref, number):
        to_left = pltpu.make_async_remote_copy(
            src_ref=ref.at[pl.ds(2, 2)],
            dst_ref=ref.at[pl.ds(width + 2, 2)],
            send_sem=send_sem.at[number, 0],
            recv_sem=recv_sem.at[number, 0],
            device_id={"blk": me - 1},
            device_id_type=MESH,
        )
        to_right = pltpu.make_async_remote_copy(
            src_ref=ref.at[pl.ds(width, 2)],
            dst_ref=ref.at[pl.ds(0, 2)],
            send_sem=send_sem.at[number, 1],
            recv_sem=recv_sem.at[number, 1],
            device_id={"blk": me + 1},
            device_id_type=MESH,
        )
        return to_left, to_right

    def send_edges(ref, number):
        to_left, to_right = edges(ref, number)
        pl.when(has_left)(lambda: to_left.start())
        pl.when(has_right)(lambda: to_right.start())

    def wait_edges(ref, number):
        to_left, to_right = edges(ref, number)
        pl.when(has_left)(lambda: to_left.wait_send())
        pl.when(has_right)(lambda: to_right.wait_send())
        pl.when(has_right)(lambda: to_left.wait_recv())
        pl.when(has_left)(lambda: to_right.wait_recv())

    for copy in local:
        copy.wait()

    @pl.loop(0, height // part)
    def _(c):
        rows = pl.ds(pl.multiple_of(c * part, part), part)
        x0[pl.ds(2, width), rows, pl.ds(0, hd)] = jnp.swapaxes(
            hidden_ref[rows].astype(f32), 0, 1
        ).astype(bf16)

    for c in chunks:

        @pl.when(has_prev)
        def _(c=c):
            onward(c).wait_recv()
            pl.when(has_next)(lambda: further(c).start())
            pl.when(odd == 0)(lambda: band_copy(2, 3, 3, c, mate).start())
            pl.when(odd == 1)(lambda: band_copy(2, 2, 1, c, mate).start())

    @pl.loop(0, height // part)
    def _(c):
        rows = pl.ds(pl.multiple_of(c * part, part), part)
        for gate in range(3):
            ctx0[gate, :, rows] = jnp.swapaxes(context_ref[gate, rows].astype(f32), 0, 1)

    deep = narrow_ref.shape[3]
    tail = deep // 16 * 16
    for section in range(2):
        for gate in range(3):
            for k in range(taps):
                weights_ref[section, gate, k, pl.ds(0, tail)] = narrow_ref[section, gate, k, pl.ds(0, tail)]
                rest = narrow_ref[section, gate, k, pl.ds(tail, deep - tail)].astype(f32)
                blank = jnp.zeros((2 * hd - deep, hd), f32)
                weights_ref[section, gate, k, pl.ds(tail, 2 * hd - tail)] = jnp.concatenate(
                    [rest, blank], axis=0
                ).astype(bf16)

    near_in = (odd == 1) | has_prev
    third_in = ((odd == 1) & has_prev) | ((odd == 0) & has_far)
    near_out = (odd == 0) | has_prev
    third_out = ((odd == 0) & has_prev) | ((odd == 1) & has_far)
    offset = offset_ref[0]
    for c in range(BAND_CHUNKS + 1):
        if c < BAND_CHUNKS:

            @pl.when(has_far)
            def _(c=c):
                further(c).wait_recv()
                pl.when(odd == 1)(lambda: band_copy(4, 3, 3, c, mate).start())

        if c >= 1:
            pl.when(near_in)(lambda c=c: band_copy(None, 2, 1, c - 1, mate).wait_recv())
            pl.when(third_in)(lambda c=c: band_copy(2, 3, 3, c - 1, mate).wait_recv())
            rows = pl.ds((c - 1) * band_rows, band_rows)
            slots = [band[slot, rows] for slot in range(5)]
            low, high = slots[1], slots[0]
            for shift in range(1, 4):
                low = jnp.where(offset == shift, slots[shift + 1], low)
                high = jnp.where(offset == shift, slots[shift], high)
            window = jnp.concatenate([low, high], axis=1)
            scores = jnp.einsum("hxc,hjc->hxj", left_ref[rows], window, preferred_element_type=f32)
            scores = jnp.swapaxes(scores, 0, 1)
            high = scores.astype(bf16).astype(f32)
            corr[:, rows] = jnp.concatenate([high, scores - high], axis=-1)

    @pl.loop(0, width // part)
    def _(c):
        cols = pl.ds(pl.multiple_of(c * part, part), part)
        feats = jnp.einsum(
            "xhj,xjf->xhf", corr[cols].astype(bf16), table_ref[cols], preferred_element_type=f32
        )
        x0[pl.ds(2 + c * part, part), :, pl.ds(hd, hd)] = feats.astype(bf16)
        x1[pl.ds(2, height), cols, pl.ds(hd, hd)] = jnp.swapaxes(feats, 0, 1).astype(bf16)

    send_edges(x0, 0)
    wait_edges(x0, 0)

    def gates(section, x, rx, z, r, context, c):
        total = None
        for k in range(taps):
            w = jnp.concatenate([weights_ref[section, 0, k], weights_ref[section, 1, k]], axis=1)
            term = jnp.dot(flat(x[pl.ds(c * part + k, part)]), w, preferred_element_type=f32)
            total = term if total is None else total + term
        shape = (part,) + x.shape[1:2] + (hd,)
        here = pl.ds(c * part, part)
        z[here] = jax.nn.sigmoid(total[:, :hd].reshape(shape) + context(0, here))
        reset = jax.nn.sigmoid(total[:, hd:].reshape(shape) + context(1, here))
        r[here] = reset
        own = x[pl.ds(c * part + 2, part), :, pl.ds(0, hd)].astype(f32)
        rx[pl.ds(c * part + 2, part)] = (reset * own).astype(bf16)

    def gated(x, rx, first):
        there = pl.ds(first, part)
        return jnp.concatenate([flat(rx[there]), flat(x[there, :, pl.ds(hd, hd)])], axis=1)

    def candidate(section, x, rx, context, c):
        total = None
        for k in range(taps):
            term = jnp.dot(
                gated(x, rx, c * part + k), weights_ref[section, 2, k], preferred_element_type=f32
            )
            total = term if total is None else total + term
        shape = (part,) + x.shape[1:2] + (hd,)
        return jnp.tanh(total.reshape(shape) + context(2, pl.ds(c * part, part)))

    def context_h(gate, here):
        return ctx0[gate, here]

    def context_v(gate, here):
        return context_ref[gate, here].astype(f32)

    @pl.loop(0, width // part)
    def _(c):
        gates(0, x0, rx0, z0, r0, context_h, c)

    send_edges(rx0, 1)
    wait_edges(rx0, 1)

    @pl.loop(0, width // part)
    def _(c):
        here = pl.ds(c * part, part)
        q = candidate(0, x0, rx0, context_h, c)
        q0[here] = q
        z = z0[here]
        own = x0[pl.ds(c * part + 2, part), :, pl.ds(0, hd)].astype(f32)
        blended = (1.0 - z) * own + z * q
        cols = pl.ds(pl.multiple_of(c * part, part), part)
        x1[pl.ds(2, height), cols, pl.ds(0, hd)] = jnp.swapaxes(blended, 0, 1).astype(bf16)

    @pl.loop(0, height // part)
    def _(c):
        gates(1, x1, rx1, z1, r1, context_v, c)

    def deltas(g, z, q, own, dq, dzr, inner):
        dq[inner] = (g * z * (1.0 - q * q)).astype(bf16)
        dzr[inner, :, pl.ds(0, hd)] = (g * (q - own) * z * (1.0 - z)).astype(bf16)

    @pl.loop(0, height // part)
    def _(c):
        here = pl.ds(c * part, part)
        inner = pl.ds(c * part + 2, part)
        q = candidate(1, x1, rx1, context_v, c)
        z = z1[here]
        own = x1[inner, :, pl.ds(0, hd)].astype(f32)
        new_ref[here] = ((1.0 - z) * own + z * q).astype(bf16)
        deltas(grad_ref[here], z, q, own, dq1, dzr1, inner)

    def back_reset(section, x, g, z, r, dq, dzr, c):
        here = pl.ds(c * part, part)
        inner = pl.ds(c * part + 2, part)
        total = None
        for k in range(taps):
            term = lax.dot_general(
                flat(dq[pl.ds(c * part + taps - 1 - k, part)]),
                weights_ref[section, 2, k, pl.ds(0, hd)],
                NT,
                preferred_element_type=f32,
            )
            total = term if total is None else total + term
        total = total.reshape((part,) + x.shape[1:2] + (hd,))
        reset = r[here]
        own = x[inner, :, pl.ds(0, hd)].astype(f32)
        dzr[inner, :, pl.ds(hd, hd)] = (total * own * reset * (1.0 - reset)).astype(bf16)
        r[here] = g[here] * (1.0 - z[here]) + total * reset

    def back_hidden(section, r, dzr, c):
        total = None
        for k in range(taps):
            w = jnp.concatenate(
                [
                    weights_ref[section, 0, k, pl.ds(0, hd)],
                    weights_ref[section, 1, k, pl.ds(0, hd)],
                ],
                axis=1,
            )
            term = lax.dot_general(
                flat(dzr[pl.ds(c * part + taps - 1 - k, part)]), w, NT, preferred_element_type=f32
            )
            total = term if total is None else total + term
        total = total.reshape((part,) + dzr.shape[1:2] + (hd,))
        return r[pl.ds(c * part, part)] + total

    def weight_grads_zr(section, x, dzr, blocks):
        acc[...] = jnp.zeros_like(acc)

        @pl.loop(0, blocks)
        def _(c):
            d = flat(dzr[pl.ds(c * part + 2, part)]).astype(f32).T.astype(bf16)
            for k in range(taps):
                acc[k] += jnp.dot(d, flat(x[pl.ds(c * part + k, part)]), preferred_element_type=f32)

        for k in range(taps):
            for gate in range(2):
                place = (gate * taps + k) * piece
                g_ref[section, pl.ds(place, piece)] = acc[k, pl.ds(gate * hd, hd)].T[:piece]

    def weight_grads_q(section, x, rx, dq, blocks):
        half = pl.ds(0, hd)
        acc[:, half] = jnp.zeros((taps, hd, 2 * hd), f32)

        @pl.loop(0, blocks)
        def _(c):
            d = flat(dq[pl.ds(c * part + 2, part)]).astype(f32).T.astype(bf16)
            for k in range(taps):
                acc[k, half] += jnp.dot(d, gated(x, rx, c * part + k), preferred_element_type=f32)

        for k in range(taps):
            place = (2 * taps + k) * piece
            g_ref[section, pl.ds(place, piece)] = acc[k, half].T[:piece]

    @pl.loop(0, height // part)
    def _(c):
        back_reset(1, x1, grad_ref, z1, r1, dq1, dzr1, c)

    @pl.loop(0, height // part)
    def _(c):
        rows = pl.ds(pl.multiple_of(c * part, part), part)
        g0[:, rows] = jnp.swapaxes(back_hidden(1, r1, dzr1, c), 0, 1)

    @pl.loop(0, width // part)
    def _(c):
        here = pl.ds(c * part, part)
        inner = pl.ds(c * part + 2, part)
        own = x0[inner, :, pl.ds(0, hd)].astype(f32)
        deltas(g0[here], z0[here], q0[here], own, dq0, dzr0, inner)

    total_rows = g_ref.shape[1]
    used = 3 * taps * piece
    if used < total_rows:
        for section in range(2):
            g_ref[section, pl.ds(used, total_rows - used)] = jnp.zeros((total_rows - used, hd), f32)

    depth = len(steps)
    spans = [(0, total_rows)]
    for k in range(depth):
        first, length = spans[-1]
        share = length // steps[k][2]
        spans.append((pl.multiple_of(first + ranks[k] * share, 16), share))
    landing = [0]
    for k in range(depth):
        landing.append(landing[-1] + spans[k][1] - spans[k + 1][1])

    def away(step, d):
        axis, stride, members = steps[step]
        target = lax.rem(partners[step][d][0] // stride, members)
        first, _ = spans[step]
        share = spans[step + 1][1]
        return pl.ds(pl.multiple_of(first + target * share, 16), share)

    def sum_copies(section, k):
        step = k if k < depth else 2 * depth - 1 - k
        copies = []
        for d in range(1, steps[step][2]):
            share = spans[step + 1][1]
            if k < depth:
                src = sbuf.at[section, away(step, d)]
                dst = rbuf.at[section, pl.ds(landing[step] + (d - 1) * share, share)]
            else:
                src = dst = sum_ref.at[section, pl.ds(spans[step + 1][0], share)]
            place, axis = partners[step][d]
            copies.append(
                pltpu.make_async_remote_copy(
                    src_ref=src,
                    dst_ref=dst,
                    send_sem=sum_send.at[section, k, d],
                    recv_sem=sum_recv.at[section, k, d],
                    device_id={axis: place},
                    device_id_type=MESH,
                )
            )
        return copies

    def begin(section, k):
        copies = sum_copies(section, k)
        for d in range(1, len(copies) + 1):
            if k < depth:
                there = away(k, d)
                sbuf[section, there] = g_ref[section, there].astype(bf16)
            copies[d - 1].start()

    def finish(section, k):
        for copy in sum_copies(section, k):
            copy.wait()
        if k < depth:
            keep, share = spans[k + 1]
            here = pl.ds(keep, share)
            summed = g_ref[section, here]
            for d in range(1, steps[k][2]):
                landed = rbuf[section, pl.ds(landing[k] + (d - 1) * share, share)]
                summed = summed + landed.astype(f32)
            if k == depth - 1:
                sum_ref[section, here] = summed.astype(bf16)
            else:
                g_ref[section, here] = summed

    def turn(section, k):
        if k >= 0:
            finish(section, k)
        if k + 1 < 2 * depth:
            begin(section, k + 1)

    send_edges(dq0, 2)
    weight_grads_zr(1, x1, dzr1, height // part)
    weight_grads_q(1, x1, rx1, dq1, height // part)
    turn(1, -1)
    wait_edges(dq0, 2)

    @pl.loop(0, width // part)
    def _(c):
        back_reset(0, x0, g0, z0, r0, dq0, dzr0, c)

    send_edges(dzr0, 3)
    turn(1, 0)
    weight_grads_q(0, x0, rx0, dq0, width // part)
    turn(1, 1)
    weight_grads_zr(0, x0, dzr0, width // part)
    turn(0, -1)
    turn(1, 2)
    wait_edges(dzr0, 3)

    @pl.loop(0, width // part)
    def _(c):
        cols = pl.ds(pl.multiple_of(c * part, part), part)
        hidden_back_ref[:, cols] = jnp.swapaxes(back_hidden(0, r0, dzr0, c), 0, 1)

    for k in range(2 * depth):
        if k + 3 < 2 * depth:
            turn(1, k + 3)
        turn(0, k)

    for c in chunks:
        pl.when(has_next)(lambda c=c: onward(c).wait_send())
        pl.when(has_next & has_prev)(lambda c=c: further(c).wait_send())
        pl.when(near_out)(lambda c=c: band_copy(None, 2, 1, c, mate).wait_send())
        pl.when(third_out)(lambda c=c: band_copy(2, 3, 3, c, mate).wait_send())


def core(offset, block, left, table, hidden, context, weights, hidden_grad, pairs, count, piece, sum_rows):
    height, width, hd = hidden.shape
    taps = weights.shape[2]
    bf16, f32 = jnp.bfloat16, jnp.float32
    vmem = pl.BlockSpec(memory_space=pltpu.VMEM)
    anywhere = pl.BlockSpec(memory_space=pl.ANY)
    steps = sum_steps(pairs, count)
    narrow = weights.shape

    def held(values):
        return pltpu.VMEM(values.shape, values.dtype)

    across = (width, height, hd)
    down = (height, width, hd)

    def padded(shape, wide):
        return pltpu.VMEM((shape[0] + 4, shape[1], wide * hd), bf16)

    return pl.pallas_call(
        functools.partial(core_kernel, count, piece, steps),
        out_shape=(
            jax.ShapeDtypeStruct(hidden.shape, bf16),
            jax.ShapeDtypeStruct(hidden.shape, f32),
            jax.ShapeDtypeStruct((2, sum_rows, hd), bf16),
        ),
        in_specs=[pl.BlockSpec(memory_space=pltpu.SMEM)] + [anywhere] * 7,
        out_specs=(vmem,) * 3,
        scratch_shapes=[
            pltpu.VMEM((5,) + block.shape, bf16),
            held(left),
            held(table),
            held(hidden),
            held(context),
            held(weights),
            held(hidden_grad),
            pltpu.VMEM(narrow[:3] + (2 * hd, hd), bf16),
            pltpu.VMEM((2, sum_rows, hd), f32),
            pltpu.VMEM((2, sum_rows, hd), bf16),
            pltpu.VMEM((2, sum_rows, hd), bf16),
            pltpu.VMEM((width, height, 4 * width), f32),
            padded(across, 2),
            padded(down, 2),
            padded(across, 1),
            padded(down, 1),
            padded(across, 1),
            padded(down, 1),
            padded(across, 2),
            padded(down, 2),
            pltpu.VMEM((3,) + across, f32),
            pltpu.VMEM(across, f32),
            pltpu.VMEM(across, f32),
            pltpu.VMEM(across, f32),
            pltpu.VMEM(down, f32),
            pltpu.VMEM(down, f32),
            pltpu.VMEM(across, f32),
            pltpu.VMEM((taps, 2 * hd, 2 * hd), f32),
            pltpu.SemaphoreType.DMA((4, 2)),
            pltpu.SemaphoreType.DMA((4, 2)),
            pltpu.SemaphoreType.DMA((4, BAND_CHUNKS)),
            pltpu.SemaphoreType.DMA((4, BAND_CHUNKS)),
            pltpu.SemaphoreType.DMA((2, 2 * len(steps), 8)),
            pltpu.SemaphoreType.DMA((2, 2 * len(steps), 8)),
            pltpu.SemaphoreType.DMA((7,)),
        ],
        compiler_params=pltpu.CompilerParams(
            collective_id=0, has_side_effects=True, vmem_limit_bytes=58 * 1024 * 1024
        ),
        name="core",
    )(offset, block, left, table, hidden, context, weights, hidden_grad)


def on_device(left_feats, right_feats, offsets, hidden, context, gru_weights, hidden_grad):
    left_block = left_feats[0]
    right_block = right_feats[0]
    column_count = left_block.shape[1]
    table = lookup_table(column_count, LEVELS, RADIUS) / math.sqrt(left_block.shape[-1])
    hd = gru_weights.shape[-1]
    table = np.concatenate([table, table], axis=1)
    table = np.pad(table, ((0, 0), (0, 0), (0, hd - table.shape[2])))
    table = jnp.asarray(table, jnp.bfloat16)
    pairs, blks = lax.axis_size("pair"), lax.axis_size("blk")
    shape = gru_weights.shape
    piece = -(-shape[3] // 8) * 8
    used = math.prod(shape[1:3]) * piece
    new_hidden, hidden_back, summed = core(
        offsets,
        right_block,
        left_block,
        table,
        hidden[0],
        context[0],
        gru_weights,
        hidden_grad[0],
        pairs,
        blks,
        piece,
        sum_rows_count(used, pairs * blks),
    )
    summed = summed[:, :used].reshape(shape[:3] + (piece, hd))
    grad_stack = summed[:, :, :, : shape[3]].astype(jnp.float32)
    return (new_hidden[None], grad_stack, hidden_back[None])


def solution(mesh):
    placed = (
        P("pair", None, "blk", None),
        P("pair", None, "blk", None),
        P("blk"),
        P("pair", None, "blk", None),
        P("pair", None, None, "blk", None),
        P(),
        P("pair", None, "blk", None),
    )
    return jax.shard_map(
        on_device,
        mesh=mesh,
        in_specs=placed,
        out_specs=(P("pair", None, "blk", None), P(), P("pair", None, "blk", None)),
        check_vma=False,
    )
```

```python
import functools
import math

import jax
import jax.numpy as jnp
import numpy as np
from jax import lax
from jax.experimental import pallas as pl
from jax.experimental.pallas import tpu as pltpu
from jax.sharding import PartitionSpec as P

LEVELS = 4
RADIUS = 4


def lookup_table(column_count, level_count, radius_len):
    tap_count = 2 * radius_len + 1
    lookup = np.zeros((column_count, 2 * column_count, level_count * tap_count), np.float32)
    positions = np.arange(column_count)
    for level_id in range(level_count):
        pool_span = 2**level_id
        pooled_cols = 2 * column_count // pool_span
        for tap_id in range(tap_count):
            centre = (positions + column_count // 2) // pool_span + tap_id - radius_len
            inside = (centre >= 0) & (centre < pooled_cols)
            for inner_id in range(pool_span):
                lookup[
                    positions[inside],
                    centre[inside] * pool_span + inner_id,
                    level_id * tap_count + tap_id,
                ] = (
                    1.0 / pool_span
                )
    return lookup


MESH = pl.DeviceIdType.MESH
BAND_CHUNKS = 8


def sum_steps(pairs, blks):
    steps = []
    for axis, size, most in (("pair", pairs, 2), ("blk", blks, 8)):
        stride = 1
        while stride < size:
            members = min(most, size // stride)
            steps.append((axis, stride, members))
            stride *= members
    return steps


def sum_rows_count(used, devices):
    step = devices * 16
    return -(-used // step) * step


NT = (((1,), (1,)), ((), ()))


def flat(values):
    return values.reshape(-1, values.shape[-1])


def core_kernel(
    count,
    piece,
    steps,
    offset_ref,
    block_in,
    left_in,
    table_in,
    hidden_in,
    context_in,
    weights_in,
    grad_in,
    new_ref,
    hidden_back_ref,
    sum_ref,
    band,
    left_ref,
    table_ref,
    hidden_ref,
    context_ref,
    narrow_ref,
    grad_ref,
    weights_ref,
    g_ref,
    sbuf,
    rbuf,
    corr,
    x0,
    x1,
    rx0,
    rx1,
    dq0,
    dq1,
    dzr0,
    dzr1,
    ctx0,
    z0,
    r0,
    q0,
    z1,
    r1,
    g0,
    acc,
    send_sem,
    recv_sem,
    band_send,
    band_recv,
    sum_send,
    sum_recv,
    local_sem,
):
    height, width, hd = hidden_ref.shape
    taps = weights_ref.shape[2]
    me = lax.axis_index("blk")
    has_left = me >= 1
    has_right = me + 1 < count
    bf16, f32 = jnp.bfloat16, jnp.float32
    part = 16

    for ref in (x0, x1, rx0, rx1, dq0, dq1, dzr0, dzr1):
        edge = jnp.zeros((2,) + ref.shape[1:], bf16)
        ref[pl.ds(0, 2)] = edge
        ref[pl.ds(ref.shape[0] - 2, 2)] = edge

    for distance in range(1, 5):

        @pl.when(me < distance)
        def _(distance=distance):
            band[distance] = jnp.zeros(band.shape[1:], bf16)

    barrier = pltpu.get_barrier_semaphore()
    places = {"pair": lax.axis_index("pair"), "blk": me}
    ranks = []
    partners = []
    for axis, stride, members in steps:
        place = places[axis]
        ranks.append(lax.rem(place // stride, members))
        row = [None]
        for d in range(1, members):
            shift = 0
            mask = 1
            while mask < members:
                if d & mask:
                    bit = lax.rem(place // (stride * mask), 2)
                    shift = shift + stride * mask * (1 - 2 * bit)
                mask *= 2
            row.append((place + shift, axis))
            pl.semaphore_signal(barrier, inc=1, device_id={axis: place + shift}, device_id_type=MESH)
        partners.append(row)
    has_next = me + 2 < count
    has_prev = me >= 2
    has_far = me >= 4
    expected = sum(members - 1 for _, _, members in steps)
    for present, shift in ((has_left, -1), (has_right, 1), (has_prev, -2), (has_next, 2)):

        @pl.when(present)
        def _(shift=shift):
            pl.semaphore_signal(barrier, inc=1, device_id={"blk": me + shift}, device_id_type=MESH)

        expected = expected + present.astype(jnp.int32)
    pl.semaphore_wait(barrier, expected)

    odd = lax.rem(me, 2)
    mate = me + 1 - 2 * odd
    band_rows = height // BAND_CHUNKS

    def band_copy(source, kind, slot, chunk, target):
        part = pl.ds(chunk * band_rows, band_rows)
        src = block_in.at[part] if source is None else band.at[source, part]
        return pltpu.make_async_remote_copy(
            src_ref=src,
            dst_ref=band.at[slot, part],
            send_sem=band_send.at[kind, chunk],
            recv_sem=band_recv.at[slot - 1, chunk],
            device_id={"blk": target},
            device_id_type=MESH,
        )

    def onward(chunk):
        return band_copy(None, 0, 2, chunk, me + 2)

    def further(chunk):
        return band_copy(2, 1, 4, chunk, me + 2)

    chunks = range(BAND_CHUNKS)
    for c in chunks:
        pl.when(has_next)(lambda c=c: onward(c).start())
        pl.when(odd == 0)(lambda c=c: band_copy(None, 2, 1, c, mate).start())

    local = [
        pltpu.make_async_copy(src, dst, local_sem.at[i])
        for i, (src, dst) in enumerate(
            (
                (hidden_in, hidden_ref),
                (context_in, context_ref),
                (weights_in, narrow_ref),
                (left_in, left_ref),
                (block_in, band.at[0]),
                (table_in, table_ref),
                (grad_in, grad_ref),
            )
        )
    ]
    for copy in local:
        copy.start()

    def edges(ref, number):
        to_left = pltpu.make_async_remote_copy(
            src_ref=ref.at[pl.ds(2, 2)],
            dst_ref=ref.at[pl.ds(width + 2, 2)],
            send_sem=send_sem.at[number, 0],
            recv_sem=recv_sem.at[number, 0],
            device_id={"blk": me - 1},
            device_id_type=MESH,
        )
        to_right = pltpu.make_async_remote_copy(
            src_ref=ref.at[pl.ds(width, 2)],
            dst_ref=ref.at[pl.ds(0, 2)],
            send_sem=send_sem.at[number, 1],
            recv_sem=recv_sem.at[number, 1],
            device_id={"blk": me + 1},
            device_id_type=MESH,
        )
        return to_left, to_right

    def send_edges(ref, number):
        to_left, to_right = edges(ref, number)
        pl.when(has_left)(lambda: to_left.start())
        pl.when(has_right)(lambda: to_right.start())

    def wait_edges(ref, number):
        to_left, to_right = edges(ref, number)
        pl.when(has_left)(lambda: to_left.wait_send())
        pl.when(has_right)(lambda: to_right.wait_send())
        pl.when(has_right)(lambda: to_left.wait_recv())
        pl.when(has_left)(lambda: to_right.wait_recv())

    for copy in local:
        copy.wait()

    @pl.loop(0, height // part)
    def _(c):
        rows = pl.ds(pl.multiple_of(c * part, part), part)
        x0[pl.ds(2, width), rows, pl.ds(0, hd)] = jnp.swapaxes(
            hidden_ref[rows].astype(f32), 0, 1
        ).astype(bf16)

    for c in chunks:

        @pl.when(has_prev)
        def _(c=c):
            onward(c).wait_recv()
            pl.when(has_next)(lambda: further(c).start())
            pl.when(odd == 0)(lambda: band_copy(2, 3, 3, c, mate).start())
            pl.when(odd == 1)(lambda: band_copy(2, 2, 1, c, mate).start())

    @pl.loop(0, height // part)
    def _(c):
        rows = pl.ds(pl.multiple_of(c * part, part), part)
        for gate in range(3):
            ctx0[gate, :, rows] = jnp.swapaxes(context_ref[gate, rows].astype(f32), 0, 1)

    deep = narrow_ref.shape[3]
    tail = deep // 16 * 16
    for section in range(2):
        for gate in range(3):
            for k in range(taps):
                weights_ref[section, gate, k, pl.ds(0, tail)] = narrow_ref[section, gate, k, pl.ds(0, tail)]
                rest = narrow_ref[section, gate, k, pl.ds(tail, deep - tail)].astype(f32)
                blank = jnp.zeros((2 * hd - deep, hd), f32)
                weights_ref[section, gate, k, pl.ds(tail, 2 * hd - tail)] = jnp.concatenate(
                    [rest, blank], axis=0
                ).astype(bf16)

    near_in = (odd == 1) | has_prev
    third_in = ((odd == 1) & has_prev) | ((odd == 0) & has_far)
    near_out = (odd == 0) | has_prev
    third_out = ((odd == 0) & has_prev) | ((odd == 1) & has_far)
    offset = offset_ref[0]
    for c in range(BAND_CHUNKS + 1):
        if c < BAND_CHUNKS:

            @pl.when(has_far)
            def _(c=c):
                further(c).wait_recv()
                pl.when(odd == 1)(lambda: band_copy(4, 3, 3, c, mate).start())

        if c >= 1:
            pl.when(near_in)(lambda c=c: band_copy(None, 2, 1, c - 1, mate).wait_recv())
            pl.when(third_in)(lambda c=c: band_copy(2, 3, 3, c - 1, mate).wait_recv())
            rows = pl.ds((c - 1) * band_rows, band_rows)
            slots = [band[slot, rows] for slot in range(5)]
            low, high = slots[1], slots[0]
            for shift in range(1, 4):
                low = jnp.where(offset == shift, slots[shift + 1], low)
                high = jnp.where(offset == shift, slots[shift], high)
            window = jnp.concatenate([low, high], axis=1)
            scores = jnp.einsum("hxc,hjc->hxj", left_ref[rows], window, preferred_element_type=f32)
            scores = jnp.swapaxes(scores, 0, 1)
            high = scores.astype(bf16).astype(f32)
            corr[:, rows] = jnp.concatenate([high, scores - high], axis=-1)

    @pl.loop(0, width // part)
    def _(c):
        cols = pl.ds(pl.multiple_of(c * part, part), part)
        feats = jnp.einsum(
            "xhj,xjf->xhf", corr[cols].astype(bf16), table_ref[cols], preferred_element_type=f32
        )
        x0[pl.ds(2 + c * part, part), :, pl.ds(hd, hd)] = feats.astype(bf16)
        x1[pl.ds(2, height), cols, pl.ds(hd, hd)] = jnp.swapaxes(feats, 0, 1).astype(bf16)

    send_edges(x0, 0)
    wait_edges(x0, 0)

    def gates(section, x, rx, z, r, context, c):
        total = None
        for k in range(taps):
            w = jnp.concatenate([weights_ref[section, 0, k], weights_ref[section, 1, k]], axis=1)
            term = jnp.dot(flat(x[pl.ds(c * part + k, part)]), w, preferred_element_type=f32)
            total = term if total is None else total + term
        shape = (part,) + x.shape[1:2] + (hd,)
        here = pl.ds(c * part, part)
        z[here] = jax.nn.sigmoid(total[:, :hd].reshape(shape) + context(0, here))
        reset = jax.nn.sigmoid(total[:, hd:].reshape(shape) + context(1, here))
        r[here] = reset
        own = x[pl.ds(c * part + 2, part), :, pl.ds(0, hd)].astype(f32)
        rx[pl.ds(c * part + 2, part)] = (reset * own).astype(bf16)

    def gated(x, rx, first):
        there = pl.ds(first, part)
        return jnp.concatenate([flat(rx[there]), flat(x[there, :, pl.ds(hd, hd)])], axis=1)

    def candidate(section, x, rx, context, c):
        total = None
        for k in range(taps):
            term = jnp.dot(
                gated(x, rx, c * part + k), weights_ref[section, 2, k], preferred_element_type=f32
            )
            total = term if total is None else total + term
        shape = (part,) + x.shape[1:2] + (hd,)
        return jnp.tanh(total.reshape(shape) + context(2, pl.ds(c * part, part)))

    def context_h(gate, here):
        return ctx0[gate, here]

    def context_v(gate, here):
        return context_ref[gate, here].astype(f32)

    @pl.loop(0, width // part)
    def _(c):
        gates(0, x0, rx0, z0, r0, context_h, c)

    send_edges(rx0, 1)
    wait_edges(rx0, 1)

    @pl.loop(0, width // part)
    def _(c):
        here = pl.ds(c * part, part)
        q = candidate(0, x0, rx0, context_h, c)
        q0[here] = q
        z = z0[here]
        own = x0[pl.ds(c * part + 2, part), :, pl.ds(0, hd)].astype(f32)
        blended = (1.0 - z) * own + z * q
        cols = pl.ds(pl.multiple_of(c * part, part), part)
        x1[pl.ds(2, height), cols, pl.ds(0, hd)] = jnp.swapaxes(blended, 0, 1).astype(bf16)

    @pl.loop(0, height // part)
    def _(c):
        gates(1, x1, rx1, z1, r1, context_v, c)

    def deltas(g, z, q, own, dq, dzr, inner):
        dq[inner] = (g * z * (1.0 - q * q)).astype(bf16)
        dzr[inner, :, pl.ds(0, hd)] = (g * (q - own) * z * (1.0 - z)).astype(bf16)

    @pl.loop(0, height // part)
    def _(c):
        here = pl.ds(c * part, part)
        inner = pl.ds(c * part + 2, part)
        q = candidate(1, x1, rx1, context_v, c)
        z = z1[here]
        own = x1[inner, :, pl.ds(0, hd)].astype(f32)
        new_ref[here] = ((1.0 - z) * own + z * q).astype(bf16)
        deltas(grad_ref[here], z, q, own, dq1, dzr1, inner)

    def back_reset(section, x, g, z, r, dq, dzr, c):
        here = pl.ds(c * part, part)
        inner = pl.ds(c * part + 2, part)
        total = None
        for k in range(taps):
            term = lax.dot_general(
                flat(dq[pl.ds(c * part + taps - 1 - k, part)]),
                weights_ref[section, 2, k, pl.ds(0, hd)],
                NT,
                preferred_element_type=f32,
            )
            total = term if total is None else total + term
        total = total.reshape((part,) + x.shape[1:2] + (hd,))
        reset = r[here]
        own = x[inner, :, pl.ds(0, hd)].astype(f32)
        dzr[inner, :, pl.ds(hd, hd)] = (total * own * reset * (1.0 - reset)).astype(bf16)
        r[here] = g[here] * (1.0 - z[here]) + total * reset

    def back_hidden(section, r, dzr, c):
        total = None
        for k in range(taps):
            w = jnp.concatenate(
                [
                    weights_ref[section, 0, k, pl.ds(0, hd)],
                    weights_ref[section, 1, k, pl.ds(0, hd)],
                ],
                axis=1,
            )
            term = lax.dot_general(
                flat(dzr[pl.ds(c * part + taps - 1 - k, part)]), w, NT, preferred_element_type=f32
            )
            total = term if total is None else total + term
        total = total.reshape((part,) + dzr.shape[1:2] + (hd,))
        return r[pl.ds(c * part, part)] + total

    def weight_grads_zr(section, x, dzr, blocks):
        acc[...] = jnp.zeros_like(acc)

        @pl.loop(0, blocks)
        def _(c):
            d = flat(dzr[pl.ds(c * part + 2, part)]).astype(f32).T.astype(bf16)
            for k in range(taps):
                acc[k] += jnp.dot(d, flat(x[pl.ds(c * part + k, part)]), preferred_element_type=f32)

        for k in range(taps):
            for gate in range(2):
                place = (gate * taps + k) * piece
                g_ref[section, pl.ds(place, piece)] = acc[k, pl.ds(gate * hd, hd)].T[:piece]

    def weight_grads_q(section, x, rx, dq, blocks):
        half = pl.ds(0, hd)
        acc[:, half] = jnp.zeros((taps, hd, 2 * hd), f32)

        @pl.loop(0, blocks)
        def _(c):
            d = flat(dq[pl.ds(c * part + 2, part)]).astype(f32).T.astype(bf16)
            for k in range(taps):
                acc[k, half] += jnp.dot(d, gated(x, rx, c * part + k), preferred_element_type=f32)

        for k in range(taps):
            place = (2 * taps + k) * piece
            g_ref[section, pl.ds(place, piece)] = acc[k, half].T[:piece]

    @pl.loop(0, height // part)
    def _(c):
        back_reset(1, x1, grad_ref, z1, r1, dq1, dzr1, c)

    @pl.loop(0, height // part)
    def _(c):
        rows = pl.ds(pl.multiple_of(c * part, part), part)
        g0[:, rows] = jnp.swapaxes(back_hidden(1, r1, dzr1, c), 0, 1)

    @pl.loop(0, width // part)
    def _(c):
        here = pl.ds(c * part, part)
        inner = pl.ds(c * part + 2, part)
        own = x0[inner, :, pl.ds(0, hd)].astype(f32)
        deltas(g0[here], z0[here], q0[here], own, dq0, dzr0, inner)

    total_rows = g_ref.shape[1]
    used = 3 * taps * piece
    if used < total_rows:
        for section in range(2):
            g_ref[section, pl.ds(used, total_rows - used)] = jnp.zeros((total_rows - used, hd), f32)

    depth = len(steps)
    orders = ([0, *range(2, depth), 1], list(range(depth)))
    spans = []
    landing = []
    for order in orders:
        row = [(0, total_rows)]
        places_in = [0]
        for at in order:
            first, length = row[-1]
            share = length // steps[at][2]
            row.append((pl.multiple_of(first + ranks[at] * share, 16), share))
            places_in.append(places_in[-1] + length - share)
        spans.append(row)
        landing.append(places_in)

    def away(section, k, d):
        at = orders[section][k]
        axis, stride, members = steps[at]
        target = lax.rem(partners[at][d][0] // stride, members)
        share = spans[section][k + 1][1]
        return pl.ds(pl.multiple_of(spans[section][k][0] + target * share, 16), share)

    def sum_copies(section, k):
        step = k if k < depth else 2 * depth - 1 - k
        at = orders[section][step]
        own, share = spans[section][step + 1]
        copies = []
        for d in range(1, steps[at][2]):
            if k < depth:
                src = sbuf.at[section, away(section, step, d)]
                dst = rbuf.at[section, pl.ds(landing[section][step] + (d - 1) * share, share)]
            else:
                src = dst = sum_ref.at[section, pl.ds(own, share)]
            place, axis = partners[at][d]
            copies.append(
                pltpu.make_async_remote_copy(
                    src_ref=src,
                    dst_ref=dst,
                    send_sem=sum_send.at[section, k, d],
                    recv_sem=sum_recv.at[section, k, d],
                    device_id={axis: place},
                    device_id_type=MESH,
                )
            )
        return copies

    def begin(section, k):
        copies = sum_copies(section, k)
        for d in range(1, len(copies) + 1):
            if k < depth:
                there = away(section, k, d)
                sbuf[section, there] = g_ref[section, there].astype(bf16)
            copies[d - 1].start()

    def finish(section, k):
        for copy in sum_copies(section, k):
            copy.wait()
        if k < depth:
            keep, share = spans[section][k + 1]
            here = pl.ds(keep, share)
            summed = g_ref[section, here]
            for d in range(1, steps[orders[section][k]][2]):
                landed = rbuf[section, pl.ds(landing[section][k] + (d - 1) * share, share)]
                summed = summed + landed.astype(f32)
            if k == depth - 1:
                sum_ref[section, here] = summed.astype(bf16)
            else:
                g_ref[section, here] = summed

    def turn(section, k):
        if k >= 0:
            finish(section, k)
        if k + 1 < 2 * depth:
            begin(section, k + 1)

    send_edges(dq0, 2)
    weight_grads_zr(1, x1, dzr1, height // part)
    weight_grads_q(1, x1, rx1, dq1, height // part)
    turn(1, -1)
    wait_edges(dq0, 2)

    @pl.loop(0, width // part)
    def _(c):
        back_reset(0, x0, g0, z0, r0, dq0, dzr0, c)

    send_edges(dzr0, 3)
    turn(1, 0)
    weight_grads_q(0, x0, rx0, dq0, width // part)
    turn(1, 1)
    weight_grads_zr(0, x0, dzr0, width // part)
    turn(0, -1)
    turn(1, 2)
    wait_edges(dzr0, 3)

    @pl.loop(0, width // part)
    def _(c):
        cols = pl.ds(pl.multiple_of(c * part, part), part)
        hidden_back_ref[:, cols] = jnp.swapaxes(back_hidden(0, r0, dzr0, c), 0, 1)

    for k in range(2 * depth):
        if k + 3 < 2 * depth:
            turn(1, k + 3)
        turn(0, k)

    for c in chunks:
        pl.when(has_next)(lambda c=c: onward(c).wait_send())
        pl.when(has_next & has_prev)(lambda c=c: further(c).wait_send())
        pl.when(near_out)(lambda c=c: band_copy(None, 2, 1, c, mate).wait_send())
        pl.when(third_out)(lambda c=c: band_copy(2, 3, 3, c, mate).wait_send())


def core(offset, block, left, table, hidden, context, weights, hidden_grad, pairs, count, piece, sum_rows):
    height, width, hd = hidden.shape
    taps = weights.shape[2]
    bf16, f32 = jnp.bfloat16, jnp.float32
    vmem = pl.BlockSpec(memory_space=pltpu.VMEM)
    anywhere = pl.BlockSpec(memory_space=pl.ANY)
    steps = sum_steps(pairs, count)
    narrow = weights.shape

    def held(values):
        return pltpu.VMEM(values.shape, values.dtype)

    across = (width, height, hd)
    down = (height, width, hd)

    def padded(shape, wide):
        return pltpu.VMEM((shape[0] + 4, shape[1], wide * hd), bf16)

    return pl.pallas_call(
        functools.partial(core_kernel, count, piece, steps),
        out_shape=(
            jax.ShapeDtypeStruct(hidden.shape, bf16),
            jax.ShapeDtypeStruct(hidden.shape, f32),
            jax.ShapeDtypeStruct((2, sum_rows, hd), bf16),
        ),
        in_specs=[pl.BlockSpec(memory_space=pltpu.SMEM)] + [anywhere] * 7,
        out_specs=(vmem,) * 3,
        scratch_shapes=[
            pltpu.VMEM((5,) + block.shape, bf16),
            held(left),
            held(table),
            held(hidden),
            held(context),
            held(weights),
            held(hidden_grad),
            pltpu.VMEM(narrow[:3] + (2 * hd, hd), bf16),
            pltpu.VMEM((2, sum_rows, hd), f32),
            pltpu.VMEM((2, sum_rows, hd), bf16),
            pltpu.VMEM((2, sum_rows, hd), bf16),
            pltpu.VMEM((width, height, 4 * width), f32),
            padded(across, 2),
            padded(down, 2),
            padded(across, 1),
            padded(down, 1),
            padded(across, 1),
            padded(down, 1),
            padded(across, 2),
            padded(down, 2),
            pltpu.VMEM((3,) + across, f32),
            pltpu.VMEM(across, f32),
            pltpu.VMEM(across, f32),
            pltpu.VMEM(across, f32),
            pltpu.VMEM(down, f32),
            pltpu.VMEM(down, f32),
            pltpu.VMEM(across, f32),
            pltpu.VMEM((taps, 2 * hd, 2 * hd), f32),
            pltpu.SemaphoreType.DMA((4, 2)),
            pltpu.SemaphoreType.DMA((4, 2)),
            pltpu.SemaphoreType.DMA((4, BAND_CHUNKS)),
            pltpu.SemaphoreType.DMA((4, BAND_CHUNKS)),
            pltpu.SemaphoreType.DMA((2, 2 * len(steps), 8)),
            pltpu.SemaphoreType.DMA((2, 2 * len(steps), 8)),
            pltpu.SemaphoreType.DMA((7,)),
        ],
        compiler_params=pltpu.CompilerParams(
            collective_id=0, has_side_effects=True, vmem_limit_bytes=58 * 1024 * 1024
        ),
        name="core",
    )(offset, block, left, table, hidden, context, weights, hidden_grad)


def on_device(left_feats, right_feats, offsets, hidden, context, gru_weights, hidden_grad):
    left_block = left_feats[0]
    right_block = right_feats[0]
    column_count = left_block.shape[1]
    table = lookup_table(column_count, LEVELS, RADIUS) / math.sqrt(left_block.shape[-1])
    hd = gru_weights.shape[-1]
    table = np.concatenate([table, table], axis=1)
    table = np.pad(table, ((0, 0), (0, 0), (0, hd - table.shape[2])))
    table = jnp.asarray(table, jnp.bfloat16)
    pairs, blks = lax.axis_size("pair"), lax.axis_size("blk")
    shape = gru_weights.shape
    piece = -(-shape[3] // 8) * 8
    used = math.prod(shape[1:3]) * piece
    new_hidden, hidden_back, summed = core(
        offsets,
        right_block,
        left_block,
        table,
        hidden[0],
        context[0],
        gru_weights,
        hidden_grad[0],
        pairs,
        blks,
        piece,
        sum_rows_count(used, pairs * blks),
    )
    summed = summed[:, :used].reshape(shape[:3] + (piece, hd))
    grad_stack = summed[:, :, :, : shape[3]].astype(jnp.float32)
    return (new_hidden[None], grad_stack, hidden_back[None])


def solution(mesh):
    placed = (
        P("pair", None, "blk", None),
        P("pair", None, "blk", None),
        P("blk"),
        P("pair", None, "blk", None),
        P("pair", None, None, "blk", None),
        P(),
        P("pair", None, "blk", None),
    )
    return jax.shard_map(
        on_device,
        mesh=mesh,
        in_specs=placed,
        out_specs=(P("pair", None, "blk", None), P(), P("pair", None, "blk", None)),
        check_vma=False,
    )
```
